128 devices in a mesh: gy: 32 (over y, x_hi, z), gz: 4 (over x_lo, core).
Axes of the slice: x: 4 (x_hi: 2, x_lo: 2; x = x_hi * 2 + x_lo), y: 4, z: 4, core: 2. Of those that a mesh axis runs over, the one named last changes fastest.
Arguments:
- source: float32 [2, 256, 256, 256], P(None, 'gy', 'gz'), may hold values from -6 to 6
- contrast: float32 [256, 256, 256], P('gy', 'gz'), may hold values from 0.5 to 3
- green: float32 [2, 512, 512, 512], P(None, 'gy', 'gz'), may hold values from -6 to 6
- forward_field: float32 [2, 256, 256, 256], P(None, 'gy', 'gz'), may hold values from -6 to 6
- density: float32 [256, 256], P('gy'), may hold values from 0 to 1
- thresh_index: int32 [64, 16], P('gy'), may hold values from 0 to 2
Outputs:
- adjoint: float32 [2, 256, 256, 256], P(None, 'gy', 'gz')
- projected: float32 [256, 256], P('gy')
- gradient: float32 [256, 256], P('gy')
The draws below stay inside these ranges and needn't reach their ends.
Inputs may be any that keep to these rules, and one draw needn't show every extreme that they name: `thresh_index`: index of a tile's threshold level.
All inputs are finite; a program needn't handle non-finite values.
Results may differ from the reference program's by a relative error of at most 0.000078.
Values sent between devices are 32-bit elements; how exact they have to be, the bound alone decides.
A program may use at most 192 MiB of HBM per device.

```python
import jax
import jax.numpy as jnp
from jax import lax

NX = 256
NY = 256
NZ = 256
SLAB = 32
RADIUS = 4
TILE_Y = 4
TILE_X = 16
PX = 512
PY = 512
PZ = 512
Z0 = 112


def with_ends(entries, stream_key, low, largest):
    spot = [jax.random.randint(jax.random.fold_in(stream_key, axis), (), 0, length) for axis, length in enumerate(entries.shape)]
    longest = entries.shape.index(max(entries.shape))
    beside = spot[:longest] + [(spot[longest] + 1) % entries.shape[longest]] + spot[longest + 1:]
    return entries.at[tuple(spot)].set(low).at[tuple(beside)].set(largest)


def shard_levels(stream_key, dims, shards, least, largest):
    factor_of, own = 1.0, jax.random.fold_in(stream_key, 6)
    for dim, shards_of in shards:
        heights = jnp.exp(jax.random.uniform(jax.random.fold_in(own, dim), (shards_of,), jnp.float32, least / len(shards), largest / len(shards)))
        factor_of = factor_of * jnp.repeat(heights, dims[dim] // shards_of).reshape([-1 if axis == dim else 1 for axis in range(len(dims))])
    return factor_of


def scatter_about(own_key, shape, deviation, most, pieces=(), kind=jnp.bfloat16):
    drawn = deviation * jax.random.normal(own_key, shape, jnp.float32)
    if pieces:
        drawn = drawn * shard_levels(own_key, shape, pieces, -0.22, 0.18)
    return jnp.clip(drawn, -most, most).astype(kind)


def setup_inputs(seed: int = 0) -> dict:
    arg_keys = jax.random.split(jax.random.key(seed), 7)
    source = scatter_about(arg_keys[0], (2, NY, NZ, NX), 1.0, 6.0, ((1, 32), (2, 4)), jnp.float32)
    contrast = jnp.clip(0.5 + 2.5 * jax.random.uniform(arg_keys[1], (NY, NZ, NX), jnp.float32) ** shard_levels(arg_keys[1], (NY, NZ, NX), ((0, 32), (1, 4)), -0.2, 0.2), 0.5, 3.0)
    green = scatter_about(arg_keys[2], (2, PX, PY, PZ), 1.0, 6.0, ((1, 32), (2, 4)), jnp.float32)
    forward_field = scatter_about(arg_keys[3], (2, NY, NZ, NX), 1.0, 6.0, ((1, 32), (2, 4)), jnp.float32)
    density = jnp.clip(1.0 * jax.random.uniform(arg_keys[4], (NY, NX), jnp.float32) ** shard_levels(arg_keys[4], (NY, NX), ((0, 32),), -0.2, 0.2), 0.0, 1.0)
    thresh_index = with_ends(jax.random.randint(arg_keys[5], (NY // TILE_Y, NX // TILE_X), 0, 3), jax.random.fold_in(arg_keys[5], 1), 0, 2).astype(jnp.int32)
    return {"source": source, "contrast": contrast, "green": green, "forward_field": forward_field, "density": density, "thresh_index": thresh_index}


sharpness = 8.0
eps_gap = 11.0


def filter_matrix(count):
    cells = jnp.arange(count)
    offset = jnp.abs(cells[:, None] - cells[None, :])
    tent_weight = jnp.maximum(RADIUS + 1 - offset, 0).astype(jnp.float32)
    return tent_weight / jnp.sum(tent_weight, axis=1, keepdims=True)


def reference(source, contrast, green, forward_field, density, thresh_index):
    stimulus = lax.complex(source[0] * contrast, source[1] * contrast)
    stimulus = jnp.transpose(stimulus, (2, 0, 1))
    spectrum = jnp.fft.fft(stimulus, n=PX, axis=0)
    spectrum = jnp.fft.fft(spectrum, n=PZ, axis=2)
    spectrum = jnp.fft.fft(spectrum, n=PY, axis=1)
    spectrum = spectrum * lax.complex(green[0], green[1])
    scattered = jnp.fft.ifft(spectrum, axis=1)[:, :NY]
    scattered = jnp.fft.ifft(scattered, axis=2)[:, :, :NZ]
    scattered = jnp.fft.ifft(scattered, axis=0)[:NX]
    scattered = jnp.transpose(scattered, (1, 2, 0))
    adjoint = jnp.stack([source[0] - jnp.real(scattered), source[1] - jnp.imag(scattered)])
    slab_adjoint = adjoint[:, :, Z0:Z0 + SLAB, :]
    slab_forward = forward_field[:, :, Z0:Z0 + SLAB, :]
    sensitivity = (eps_gap / SLAB) * jnp.sum(slab_adjoint[0] * slab_forward[0] - slab_adjoint[1] * slab_forward[1], axis=1)
    highest = lax.Precision.HIGHEST
    filt_y = filter_matrix(NY)
    filt_x = filter_matrix(NX)
    filtered = jnp.dot(jnp.dot(filt_y, density, precision=highest), filt_x.T, precision=highest)
    levels = 0.35 + 0.1 * thresh_index.astype(jnp.float32)
    threshold = jnp.repeat(jnp.repeat(levels, TILE_Y, axis=0), TILE_X, axis=1)
    steepness = jnp.tanh(sharpness * (filtered - threshold))
    offset_term = jnp.tanh(sharpness * threshold)
    denominator = offset_term + jnp.tanh(sharpness * (1.0 - threshold))
    projected = (offset_term + steepness) / denominator
    weighted = sharpness * (1.0 - steepness * steepness) / denominator * sensitivity
    gradient = jnp.dot(jnp.dot(filt_y.T, weighted, precision=highest), filt_x, precision=highest)
    return adjoint, projected, gradient
```

```python
import functools

import jax
import jax.numpy as jnp
import ml_dtypes
import numpy as np
from jax import lax
from jax.experimental import pallas as pl
from jax.experimental.pallas import tpu as pltpu
from jax.sharding import PartitionSpec as P

NX = NY = NZ = 256
PAD = 512
SLAB = 32
RADIUS = 4
TILE_Y = 4
TILE_X = 16
Z0 = 112
SHARP = 8.0
GAP = 11.0

GY = 32
GZ = 4
ROWS = NY // GY
DEPTH = NZ // GZ
XF = PAD // GY
YF = PAD // GZ
LANES = 2 * DEPTH
CH = 4
CX = XF // CH

F32 = jnp.float32
BF16 = jnp.bfloat16
MESH = pl.DeviceIdType.MESH


def halves(table):
    high = table.astype(ml_dtypes.bfloat16)
    low = (table - high.astype(np.float64)).astype(ml_dtypes.bfloat16)
    return high, low


def tables():
    k = np.arange(PAD)[:, None]
    p = np.arange(NX)[None, :]
    angle = (k * p % PAD) * (2.0 * np.pi / PAD)
    cos, sin = np.cos(angle), np.sin(angle)
    order = np.arange(PAD).reshape(GY, CH, CX).transpose(1, 0, 2).reshape(CH, GY * CX)
    fx = np.concatenate([cos[order], sin[order]], axis=2)
    fy = np.concatenate([cos, sin], axis=1).reshape(GZ, YF, 2 * NY)
    fyi = np.concatenate([cos.T, -sin.T], axis=1)
    fxi = np.concatenate(
        [cos[order].transpose(0, 2, 1), -sin[order].transpose(0, 2, 1)], axis=2
    )
    c4 = cos.reshape(2, 256, GZ, DEPTH)
    s4 = sin.reshape(2, 256, GZ, DEPTH)
    ct, st = c4.transpose(0, 2, 3, 1), s4.transpose(0, 2, 3, 1)
    re_rows = np.concatenate([ct, -st], axis=3)
    im_rows = np.concatenate([st, ct], axis=3)
    wz = np.stack([re_rows, im_rows], axis=2).reshape(2, 2 * NZ, 512)
    wzi = wz.transpose(0, 2, 1).reshape(1024, 512)
    flat = []
    for table in (fx, fy, fyi, fxi, wz, wzi):
        flat.extend(halves(table))
    cells = np.arange(NX)
    tent = np.maximum(RADIUS + 1 - np.abs(cells[:, None] - cells[None, :]), 0).astype(
        np.float32
    )
    filt = tent / tent.sum(axis=1, keepdims=True)
    return flat + [filt, np.ascontiguousarray(filt.T)]


def split(value):
    high = value.astype(BF16)
    return high, (value - high.astype(F32)).astype(BF16)


def product(ah, al, bh, bl):
    dot = functools.partial(jnp.dot, preferred_element_type=F32)
    return dot(ah, bh) + dot(al, bh) + dot(ah, bl)


def turned(block, sign):
    return pltpu.roll(block, DEPTH, 1) * sign


def turned_pair(pair, sign):
    return jnp.concatenate(
        [turned(pair[:, :LANES], sign), turned(pair[:, LANES:], sign)], axis=1
    )


def kernel(*refs):
    (src_h, con_h, fwd_h, green_h, dens, level) = refs[:6]
    tabs_h = refs[6:20]
    adj, proj, grad = refs[20:23]
    (src, con, fwd, green) = refs[23:27]
    tabs = refs[27:41]
    (sth, stl, s1, r1, y1, r2, zi, r3, yi, r4, acc, bh, bl, ah, al, qh, ql) = refs[41:58]
    (near, fact, slab, slabs) = refs[58:62]
    (in_sem, tab_sem, ss1, rs1, ls1, ss2, rs2, ls2) = refs[62:70]
    (ss3, rs3, ls3, ss4, rs4, ls4, sn, rn, sf, rf, sp, rp) = refs[70:82]
    fxh, fxl, fyh, fyl, fyih, fyil, fxih, fxil, wzh, wzl, wih, wil, filt, filt_t = tabs

    me = lax.axis_index("gy")
    mz = lax.axis_index("gz")
    after, before = lax.rem(me + 1, GY), lax.rem(me + GY - 1, GY)

    slab_z = pl.multiple_of(jnp.where(mz == 1, 48, 0), 16)
    loads = [
        pltpu.make_async_copy(src_h, src, in_sem.at[0]),
        pltpu.make_async_copy(con_h, con, in_sem.at[1]),
        pltpu.make_async_copy(fwd_h.at[:, :, pl.ds(slab_z, 16), :], fwd, in_sem.at[2]),
        pltpu.make_async_copy(green_h, green, in_sem.at[3]),
    ]
    fills = [
        pltpu.make_async_copy(tabs_h[n], tabs[n], tab_sem.at[n]) for n in range(14)
    ]
    loads[0].start()
    loads[1].start()
    for n in range(12):
        fills[n].start()
    loads[3].start()
    fills[12].start()
    fills[13].start()
    loads[2].start()

    barrier = pltpu.get_barrier_semaphore()

    @pl.loop(1, GY)
    def _(k):
        pl.semaphore_signal(
            barrier, inc=1, device_id={"gy": lax.rem(me + k, GY)}, device_id_type=MESH
        )

    for k in range(1, GZ):
        other = lax.rem(mz + k, GZ)
        pl.semaphore_signal(barrier, inc=1, device_id={"gz": other}, device_id_type=MESH)
        for row in (after, before):
            pl.semaphore_signal(
                barrier,
                inc=1,
                device_id={"gy": row, "gz": other},
                device_id_type=MESH,
            )

    lane = lax.broadcasted_iota(jnp.int32, (1, LANES), 1)
    sign = jnp.where(lane < DEPTH, 1.0, -1.0).astype(F32)

    loads[0].wait()
    loads[1].wait()

    @pl.loop(0, ROWS)
    def _(y):
        weight = con[y]
        both = jnp.concatenate([src[0, y] * weight, src[1, y] * weight], axis=0)
        flat = both.T
        full = jnp.concatenate([flat, turned(flat, sign)], axis=0)
        high, low = split(full)
        sth[y] = high
        stl[y] = low

    fills[0].wait()
    fills[1].wait()

    pl.semaphore_wait(barrier, (GY - 1) + 3 * (GZ - 1))

    def near_copy(buffer, slot, target, sems, recv):
        return pltpu.make_async_remote_copy(
            src_ref=buffer.at[2],
            dst_ref=buffer.at[slot],
            send_sem=sems.at[slot],
            recv_sem=recv.at[slot],
            device_id={"gy": target},
            device_id_type=MESH,
        )

    near[2] = dens[...]
    near_copies = [near_copy(near, 0, after, sn, rn), near_copy(near, 1, before, sn, rn)]
    for copy in near_copies:
        copy.start()

    @pl.loop(0, CH)
    def _(i):
        lh, ll = fxh[i], fxl[i]
        for k in range(ROWS // 2):
            rh = jnp.concatenate([sth[2 * k], sth[2 * k + 1]], axis=1)
            rl = jnp.concatenate([stl[2 * k], stl[2 * k + 1]], axis=1)
            out = product(lh, ll, rh, rl)
            s1[i, :, 2 * k, :] = out[:, :LANES]
            s1[i, :, 2 * k + 1, :] = out[:, LANES:]

        def part(p):
            return s1.at[i, pl.ds(CX * p, CX)]

        mine = r1.at[pl.ds(CX * i, CX), pl.ds(pl.multiple_of(ROWS * me, ROWS), ROWS), :]

        @pl.loop(1, GY)
        def _(k):
            p = lax.rem(me + k, GY)
            pltpu.make_async_remote_copy(
                src_ref=part(p),
                dst_ref=mine,
                send_sem=ss1.at[i],
                recv_sem=rs1.at[i],
                device_id={"gy": p},
                device_id_type=MESH,
            ).start()

        pltpu.make_async_copy(part(me), mine, ls1.at[i]).start()

    fills[12].wait()
    fills[13].wait()
    for copy in near_copies:
        copy.wait()

    def wide(buffer):
        rows = jnp.concatenate(
            [buffer[0][ROWS - RADIUS :], buffer[2], buffer[1][:RADIUS]], axis=0
        )
        return jnp.where(inside, rows, 0.0)

    row = ROWS * me - RADIUS + lax.broadcasted_iota(jnp.int32, (2 * ROWS, NX), 0)
    inside = (row >= 0) & (row < NY)
    weight16 = jnp.zeros((2 * ROWS, NX), F32)
    for offset in range(-RADIUS, RADIUS + 1):
        valid = (row + offset >= 0) & (row + offset < NY)
        weight16 = weight16 + jnp.where(valid, float(RADIUS + 1 - abs(offset)), 0.0)

    def tent_rows(rows):
        total = jnp.zeros((ROWS, NX), F32)
        for offset in range(-RADIUS, RADIUS + 1):
            start = RADIUS + offset
            total = total + float(RADIUS + 1 - abs(offset)) * rows[start : start + ROWS]
        return total

    exact = functools.partial(
        jnp.dot, preferred_element_type=F32, precision=lax.Precision.HIGHEST
    )
    smooth = tent_rows(wide(near)) / weight16[RADIUS : RADIUS + ROWS]
    filtered = exact(smooth, filt_t[...])
    threshold = level[...]
    steep = jnp.tanh(SHARP * (filtered - threshold))
    shift = jnp.tanh(SHARP * threshold)
    below = shift + jnp.tanh(SHARP * (1.0 - threshold))
    proj[...] = (shift + steep) / below
    fact[2] = SHARP * (1.0 - steep * steep) / below
    fact_copies = [near_copy(fact, 0, after, sf, rf), near_copy(fact, 1, before, sf, rf)]
    for copy in fact_copies:
        copy.start()

    for n in range(2, 12):
        fills[n].wait()
    loads[3].wait()

    @pl.loop(0, CH)
    def _(i):
        rows = pl.ds(CX * i, CX)
        got = r1.at[rows, pl.ds(0, NY - ROWS), :]
        pltpu.make_async_copy(got, got, rs1.at[i]).wait()
        own = r1.at[rows, pl.ds(0, ROWS), :]
        pltpu.make_async_copy(own, own, ls1.at[i]).wait()

        @pl.loop(0, CX // 2)
        def _(k):
            x = CX * i + 2 * k
            pair = jnp.concatenate([r1[x], r1[x + 1]], axis=1)
            full = jnp.concatenate([pair, turned_pair(pair, sign)], axis=0)
            high, low = split(full)
            bh[: 2 * NY] = high
            bl[: 2 * NY] = low
            for d in range(GZ):
                out = product(fyh[d], fyl[d], bh[: 2 * NY], bl[: 2 * NY])
                y1[x, d * YF : (d + 1) * YF, :] = out[:, :LANES]
                y1[x + 1, d * YF : (d + 1) * YF, :] = out[:, LANES:]

        def part(d):
            return y1.at[rows, pl.ds(pl.multiple_of(YF * d, YF), YF), :]

        for k in range(1, GZ):
            d = lax.rem(mz + k, GZ)
            pltpu.make_async_remote_copy(
                src_ref=part(d),
                dst_ref=r2.at[mz, rows],
                send_sem=ss2.at[i],
                recv_sem=rs2.at[i],
                device_id={"gz": d},
                device_id_type=MESH,
            ).start()
        pltpu.make_async_copy(part(mz), r2.at[mz, rows], ls2.at[i]).start()

    @pl.loop(0, CH)
    def _(i):
        rows = pl.ds(CX * i, CX)
        got = r2.at[pl.ds(0, GZ - 1), rows]
        pltpu.make_async_copy(got, got, rs2.at[i]).wait()
        own = r2.at[0, rows]
        pltpu.make_async_copy(own, own, ls2.at[i]).wait()

        @pl.loop(0, CX // 2)
        def _(k):
            x = CX * i + 2 * k
            for j in range(2):
                line = jnp.concatenate([r2[d, x + j] for d in range(GZ)], axis=1)
                high, low = split(line)
                ah[j * YF : (j + 1) * YF] = high
                al[j * YF : (j + 1) * YF] = low
            for n in range(2):
                out = product(ah[...], al[...], wzh[n], wzl[n])
                for j in range(2):
                    lines = slice(j * YF, (j + 1) * YF)
                    real, imag = out[lines, :256], out[lines, 256:]
                    g_real = green[0, x + j, :, 256 * n : 256 * n + 256]
                    g_imag = green[1, x + j, :, 256 * n : 256 * n + 256]
                    high, low = split(real * g_real - imag * g_imag)
                    qh[lines, 512 * n : 512 * n + 256] = high
                    ql[lines, 512 * n : 512 * n + 256] = low
                    high, low = split(real * g_imag + imag * g_real)
                    qh[lines, 512 * n + 256 : 512 * n + 512] = high
                    ql[lines, 512 * n + 256 : 512 * n + 512] = low
            out = product(qh[...], ql[...], wih[...], wil[...])
            for j in range(2):
                for d in range(GZ):
                    zi[d, x + j] = out[j * YF : (j + 1) * YF, d * LANES : (d + 1) * LANES]

        mine = r3.at[rows, pl.ds(pl.multiple_of(YF * mz, YF), YF), :]
        for k in range(1, GZ):
            d = lax.rem(mz + k, GZ)
            pltpu.make_async_remote_copy(
                src_ref=zi.at[d, rows],
                dst_ref=mine,
                send_sem=ss3.at[i],
                recv_sem=rs3.at[i],
                device_id={"gz": d},
                device_id_type=MESH,
            ).start()
        pltpu.make_async_copy(zi.at[mz, rows], mine, ls3.at[i]).start()

    @pl.loop(0, CH)
    def _(i):
        rows = pl.ds(CX * i, CX)
        got = r3.at[rows, pl.ds(0, PAD - YF), :]
        pltpu.make_async_copy(got, got, rs3.at[i]).wait()
        own = r3.at[rows, pl.ds(0, YF), :]
        pltpu.make_async_copy(own, own, ls3.at[i]).wait()

        @pl.loop(0, CX // 2)
        def _(k):
            x = CX * i + 2 * k
            pair = jnp.concatenate([r3[x], r3[x + 1]], axis=1)
            full = jnp.concatenate([pair, turned_pair(pair, sign)], axis=0)
            high, low = split(full)
            bh[...] = high
            bl[...] = low
            out = product(fyih[...], fyil[...], bh[...], bl[...])
            yi[x] = out[:, :LANES]
            yi[x + 1] = out[:, LANES:]

        def part(p):
            return yi.at[rows, pl.ds(pl.multiple_of(ROWS * p, ROWS), ROWS), :]

        mine = r4.at[i, pl.ds(CX * me, CX)]

        @pl.loop(1, GY)
        def _(k):
            p = lax.rem(me + k, GY)
            pltpu.make_async_remote_copy(
                src_ref=part(p),
                dst_ref=mine,
                send_sem=ss4.at[i],
                recv_sem=rs4.at[i],
                device_id={"gy": p},
                device_id_type=MESH,
            ).start()

        pltpu.make_async_copy(part(me), mine, ls4.at[i]).start()

    acc[...] = jnp.zeros_like(acc)

    @pl.loop(0, CH)
    def _(i):
        got = r4.at[i, pl.ds(0, CX * (GY - 1))]
        pltpu.make_async_copy(got, got, rs4.at[i]).wait()
        own = r4.at[i, pl.ds(0, CX)]
        pltpu.make_async_copy(own, own, ls4.at[i]).wait()
        lh, ll = fxih[i], fxil[i]
        for k in range(ROWS // 2):
            pair = jnp.concatenate([r4[i, :, 2 * k, :], r4[i, :, 2 * k + 1, :]], axis=1)
            full = jnp.concatenate([pair, turned_pair(pair, sign)], axis=0)
            high, low = split(full)
            acc[k] += product(lh, ll, high, low)

    scale = 1.0 / float(PAD) ** 3

    @pl.loop(0, ROWS // 2)
    def _(k):
        for j in range(2):
            flat = acc[k, :, j * LANES : (j + 1) * LANES].T * scale
            adj[0, 2 * k + j] = src[0, 2 * k + j] - flat[:DEPTH]
            adj[1, 2 * k + j] = src[1, 2 * k + j] - flat[DEPTH:]

    loads[2].wait()
    holds = (mz == 1) | (mz == 2)
    slot = jnp.where(mz == 2, 1, 0)

    def slab_copy(step, turn):
        return pltpu.make_async_remote_copy(
            src_ref=slab,
            dst_ref=slabs.at[1 - step, slot],
            send_sem=sp.at[step + 1, turn],
            recv_sem=rp.at[1 - step, slot],
            device_id={
                "gy": lax.rem(me + GY + step, GY),
                "gz": lax.rem(mz + turn, GZ),
            },
            device_id_type=MESH,
        )

    reaches = [
        (step, turn) for step in (-1, 0, 1) for turn in range(GZ) if step or turn
    ]

    @pl.when(holds)
    def _():
        planes = pl.ds(slab_z, 16)
        field = adj[0, :, planes, :] * fwd[0] - adj[1, :, planes, :] * fwd[1]
        total = jnp.sum(field, axis=1) * (GAP / SLAB)
        slab[...] = total
        slabs[1, slot] = total
        for step, turn in reaches:
            slab_copy(step, turn).start()

    for copy in fact_copies:
        copy.wait()
    for step in range(3):
        for source in range(2):
            arrived = pltpu.make_async_copy(slab, slabs.at[step, source], rp.at[step, source])
            if step == 1:

                @pl.when(mz != source + 1)
                def _(arrived=arrived):
                    arrived.wait()

            else:
                arrived.wait()

    summed = [slabs[step, 0] + slabs[step, 1] for step in range(3)]
    sense = jnp.concatenate(
        [summed[0][ROWS - RADIUS :], summed[1], summed[2][:RADIUS]], axis=0
    )
    weighted = jnp.where(inside, wide(fact) * sense, 0.0)
    scaled = exact(weighted, filt[...]) / jnp.where(inside, weight16, 1.0)
    grad[...] = tent_rows(scaled)

    @pl.when(holds)
    def _():
        for step, turn in reaches:
            slab_copy(step, turn).wait_send()

    @pl.loop(0, CH)
    def _(i):
        rows = pl.ds(CX * i, CX)
        sent = s1.at[i, pl.ds(0, CX * (GY - 1))]
        pltpu.make_async_copy(sent, sent, ss1.at[i]).wait()
        sent = r2.at[pl.ds(0, GZ - 1), rows]
        pltpu.make_async_copy(sent, sent, ss2.at[i]).wait()
        sent = zi.at[pl.ds(0, GZ - 1), rows]
        pltpu.make_async_copy(sent, sent, ss3.at[i]).wait()
        sent = yi.at[rows, pl.ds(0, NY - ROWS), :]
        pltpu.make_async_copy(sent, sent, ss4.at[i]).wait()


def shards(source, contrast, green, forward_field, density, thresh_index):
    levels = 0.35 + 0.1 * thresh_index.astype(F32)
    threshold = jnp.broadcast_to(
        levels[:, None, :, None], (levels.shape[0], TILE_Y, levels.shape[1], TILE_X)
    ).reshape(ROWS, NX)
    constants = tables()
    anywhere = pl.BlockSpec(memory_space=pl.ANY)
    vmem = pl.BlockSpec(memory_space=pltpu.VMEM)
    dma = pltpu.SemaphoreType.DMA
    block = pltpu.VMEM
    scratch = [
        block((2, ROWS, DEPTH, NX), F32),
        block((ROWS, DEPTH, NX), F32),
        block((2, ROWS, 16, NX), F32),
        block((2, XF, YF, PAD), F32),
    ]
    scratch += [block(table.shape, table.dtype) for table in constants]
    scratch += [
        block((ROWS, 2 * NX, LANES), BF16),
        block((ROWS, 2 * NX, LANES), BF16),
        block((CH, GY * CX, ROWS, LANES), F32),
        block((XF, NY, LANES), F32),
        block((XF, PAD, LANES), F32),
        block((GZ, XF, YF, LANES), F32),
        block((GZ, XF, YF, LANES), F32),
        block((XF, PAD, LANES), F32),
        block((XF, NY, LANES), F32),
        block((CH, GY * CX, ROWS, LANES), F32),
        block((ROWS // 2, NX, 2 * LANES), F32),
        block((2 * PAD, 2 * LANES), BF16),
        block((2 * PAD, 2 * LANES), BF16),
        block((2 * YF, 2 * NZ), BF16),
        block((2 * YF, 2 * NZ), BF16),
        block((2 * YF, 2 * PAD), BF16),
        block((2 * YF, 2 * PAD), BF16),
        block((3, ROWS, NX), F32),
        block((3, ROWS, NX), F32),
        block((ROWS, NX), F32),
        block((3, 2, ROWS, NX), F32),
        dma((4,)),
        dma((14,)),
    ]
    scratch += [dma((CH,)) for _ in range(12)]
    scratch += [dma((2,)) for _ in range(4)]
    scratch += [dma((3, GZ)), dma((3, 2))]
    return pl.pallas_call(
        kernel,
        out_shape=(
            jax.ShapeDtypeStruct((2, ROWS, DEPTH, NX), F32),
            jax.ShapeDtypeStruct((ROWS, NX), F32),
            jax.ShapeDtypeStruct((ROWS, NX), F32),
        ),
        in_specs=[anywhere] * 4 + [vmem] * 2 + [anywhere] * 14,
        out_specs=(vmem, vmem, vmem),
        scratch_shapes=scratch,
        compiler_params=pltpu.CompilerParams(
            collective_id=0, has_side_effects=True, vmem_limit_bytes=62 << 20
        ),
    )(source, contrast, forward_field, green, density, threshold, *map(jnp.asarray, constants))


def solution(mesh):
    return jax.shard_map(
        shards,
        mesh=mesh,
        in_specs=(
            P(None, "gy", "gz", None),
            P("gy", "gz", None),
            P(None, "gy", "gz", None),
            P(None, "gy", "gz", None),
            P("gy", None),
            P("gy", None),
        ),
        out_specs=(P(None, "gy", "gz", None), P("gy", None), P("gy", None)),
        check_vma=False,
    )
```

```python
import functools

import jax
import jax.numpy as jnp
import ml_dtypes
import numpy as np
from jax import lax
from jax.experimental import pallas as pl
from jax.experimental.pallas import tpu as pltpu
from jax.sharding import PartitionSpec as P

NX = NY = NZ = 256
PAD = 512
SLAB = 32
RADIUS = 4
TILE_Y = 4
TILE_X = 16
Z0 = 112
SHARP = 8.0
GAP = 11.0

GY = 32
GZ = 4
ROWS = NY // GY
DEPTH = NZ // GZ
XF = PAD // GY
YF = PAD // GZ
LANES = 2 * DEPTH
CH = 4
CX = XF // CH

F32 = jnp.float32
BF16 = jnp.bfloat16
MESH = pl.DeviceIdType.MESH


def halves(table):
    high = table.astype(ml_dtypes.bfloat16)
    low = (table - high.astype(np.float64)).astype(ml_dtypes.bfloat16)
    return high, low


def tables():
    k = np.arange(PAD)[:, None]
    p = np.arange(NX)[None, :]
    angle = (k * p % PAD) * (2.0 * np.pi / PAD)
    cos, sin = np.cos(angle), np.sin(angle)
    order = np.arange(PAD).reshape(GY, CH, CX).transpose(1, 0, 2).reshape(CH, GY * CX)
    fx = np.concatenate([cos[order], sin[order]], axis=2)
    fy = np.concatenate([cos, sin], axis=1).reshape(GZ, YF, 2 * NY)
    half = (2, PAD // 2, NY)
    fyi = np.concatenate(
        [cos.reshape(half).transpose(0, 2, 1), -sin.reshape(half).transpose(0, 2, 1)],
        axis=2,
    )
    fxi = np.concatenate(
        [cos[order].transpose(0, 2, 1), -sin[order].transpose(0, 2, 1)], axis=2
    )
    shape = (2, 256, 2, 2, DEPTH)
    ct = cos.reshape(shape).transpose(0, 3, 2, 4, 1)
    st = sin.reshape(shape).transpose(0, 3, 2, 4, 1)
    re_rows = np.concatenate([ct, -st], axis=4)
    im_rows = np.concatenate([st, ct], axis=4)
    wz = np.stack([re_rows, im_rows], axis=3).reshape(2, 2 * NZ, 512)
    wzi = wz.transpose(0, 2, 1).reshape(1024, 512)
    flat = []
    for table in (fx, fy, fyi, fxi, wz, wzi):
        flat.extend(halves(table))
    cells = np.arange(NX)
    tent = np.maximum(RADIUS + 1 - np.abs(cells[:, None] - cells[None, :]), 0).astype(
        np.float32
    )
    filt = tent / tent.sum(axis=1, keepdims=True)
    return flat + [filt, np.ascontiguousarray(filt.T)]


def split(value):
    high = value.astype(BF16)
    return high, (value - high.astype(F32)).astype(BF16)


def product(ah, al, bh, bl):
    dot = functools.partial(jnp.dot, preferred_element_type=F32)
    return dot(ah, bh) + dot(al, bh) + dot(ah, bl)


def turned(block, sign):
    return pltpu.roll(block, DEPTH, 1) * sign


def turned_pair(pair, sign):
    return jnp.concatenate(
        [turned(pair[:, :LANES], sign), turned(pair[:, LANES:], sign)], axis=1
    )


def kernel(*refs):
    (src_h, con_h, fwd_h, green_h, dens, level) = refs[:6]
    tabs_h = refs[6:20]
    adj, proj, grad = refs[20:23]
    (src, con, fwd, green) = refs[23:27]
    tabs = refs[27:41]
    (sth, stl, s1, r1, y1, r2, zi, r3, yp, yr, yi, r4, acc) = refs[41:54]
    (bh, bl, ah, al, qh, ql, near, fact, slab, slabs) = refs[54:64]
    (in_sem, tab_sem, sn, rn, sf, rf, sp, rp) = refs[64:72]
    (ss1, rs1, ss2, rs2, ss3, rs3, ls3, ss4, rs4, ls4, ss5, rs5, ss6, rs6) = refs[72:86]
    fxh, fxl, fyh, fyl, fyih, fyil, fxih, fxil, wzh, wzl, wih, wil, filt, filt_t = tabs

    me = lax.axis_index("gy")
    mz = lax.axis_index("gz")
    after, before = lax.rem(me + 1, GY), lax.rem(me + GY - 1, GY)
    core, chip = lax.rem(mz, 2), mz // 2
    side = lax.rem(me // 4, 2)
    sibling = mz + 1 - 2 * core
    partner = lax.rem(mz + 2, GZ)

    def place(p):
        return p // 8, lax.rem(p // 4, 2), pl.multiple_of(ROWS * lax.rem(p, 4), ROWS)

    def across(p):
        same = lax.rem(p // 4, 2) == side
        return {"gy": p, "gz": jnp.where(same, mz, partner)}

    slab_z = pl.multiple_of(jnp.where(mz == 1, 48, 0), 16)
    loads = [
        pltpu.make_async_copy(src_h, src, in_sem.at[0]),
        pltpu.make_async_copy(con_h, con, in_sem.at[1]),
        pltpu.make_async_copy(fwd_h.at[:, :, pl.ds(slab_z, 16), :], fwd, in_sem.at[2]),
        pltpu.make_async_copy(green_h, green, in_sem.at[3]),
    ]
    fills = [
        pltpu.make_async_copy(tabs_h[n], tabs[n], tab_sem.at[n]) for n in range(14)
    ]
    loads[0].start()
    loads[1].start()
    for n in range(12):
        fills[n].start()
    loads[3].start()
    fills[12].start()
    fills[13].start()
    loads[2].start()

    barrier = pltpu.get_barrier_semaphore()

    @pl.loop(1, GY)
    def _(k):
        pl.semaphore_signal(
            barrier, inc=1, device_id=across(lax.rem(me + k, GY)), device_id_type=MESH
        )

    for k in range(GZ):
        other = lax.rem(mz + k, GZ)
        for row in (after, before) + ((me,) if k else ()):
            pl.semaphore_signal(
                barrier,
                inc=1,
                device_id={"gy": row, "gz": other},
                device_id_type=MESH,
            )

    lane = lax.broadcasted_iota(jnp.int32, (1, LANES), 1)
    sign = jnp.where(lane < DEPTH, 1.0, -1.0).astype(F32)

    loads[0].wait()
    loads[1].wait()

    @pl.loop(0, ROWS)
    def _(y):
        weight = con[y]
        both = jnp.concatenate([src[0, y] * weight, src[1, y] * weight], axis=0)
        flat = both.T
        full = jnp.concatenate([flat, turned(flat, sign)], axis=0)
        high, low = split(full)
        sth[y] = high
        stl[y] = low

    fills[0].wait()
    fills[1].wait()

    pl.semaphore_wait(barrier, (GY - 1) + 2 * GZ + (GZ - 1))

    def near_copy(buffer, slot, target, sems, recv):
        return pltpu.make_async_remote_copy(
            src_ref=buffer.at[2],
            dst_ref=buffer.at[slot],
            send_sem=sems.at[slot],
            recv_sem=recv.at[slot],
            device_id={"gy": target},
            device_id_type=MESH,
        )

    near[2] = dens[...]
    near_copies = [near_copy(near, 0, after, sn, rn), near_copy(near, 1, before, sn, rn)]
    for copy in near_copies:
        copy.start()

    @pl.loop(0, CH)
    def _(i):
        lh, ll = fxh[i], fxl[i]
        for k in range(ROWS // 2):
            rh = jnp.concatenate([sth[2 * k], sth[2 * k + 1]], axis=1)
            rl = jnp.concatenate([stl[2 * k], stl[2 * k + 1]], axis=1)
            out = product(lh, ll, rh, rl)
            s1[i, :, 2 * k, :] = out[:, :LANES]
            s1[i, :, 2 * k + 1, :] = out[:, LANES:]

        def part(p):
            return s1.at[i, pl.ds(CX * p, CX)]

        group, pair, first = place(me)
        mine = r1.at[chip, pl.ds(CX * i, CX), group, pair, pl.ds(first, ROWS)]

        @pl.loop(1, GY)
        def _(k):
            p = lax.rem(me + k, GY)
            pltpu.make_async_remote_copy(
                src_ref=part(p),
                dst_ref=mine,
                send_sem=ss1.at[i],
                recv_sem=rs1.at[i],
                device_id=across(p),
                device_id_type=MESH,
            ).start()

        pltpu.make_async_copy(part(me), mine, rs1.at[i]).start()

    fills[12].wait()
    fills[13].wait()
    for copy in near_copies:
        copy.wait()

    def wide(buffer):
        rows = jnp.concatenate(
            [buffer[0][ROWS - RADIUS :], buffer[2], buffer[1][:RADIUS]], axis=0
        )
        return jnp.where(inside, rows, 0.0)

    row = ROWS * me - RADIUS + lax.broadcasted_iota(jnp.int32, (2 * ROWS, NX), 0)
    inside = (row >= 0) & (row < NY)
    weight16 = jnp.zeros((2 * ROWS, NX), F32)
    for offset in range(-RADIUS, RADIUS + 1):
        valid = (row + offset >= 0) & (row + offset < NY)
        weight16 = weight16 + jnp.where(valid, float(RADIUS + 1 - abs(offset)), 0.0)

    def tent_rows(rows):
        total = jnp.zeros((ROWS, NX), F32)
        for offset in range(-RADIUS, RADIUS + 1):
            start = RADIUS + offset
            total = total + float(RADIUS + 1 - abs(offset)) * rows[start : start + ROWS]
        return total

    exact = functools.partial(
        jnp.dot, preferred_element_type=F32, precision=lax.Precision.HIGHEST
    )
    smooth = tent_rows(wide(near)) / weight16[RADIUS : RADIUS + ROWS]
    filtered = exact(smooth, filt_t[...])
    threshold = level[...]
    steep = jnp.tanh(SHARP * (filtered - threshold))
    shift = jnp.tanh(SHARP * threshold)
    below = shift + jnp.tanh(SHARP * (1.0 - threshold))
    proj[...] = (shift + steep) / below
    fact[2] = SHARP * (1.0 - steep * steep) / below
    fact_copies = [near_copy(fact, 0, after, sf, rf), near_copy(fact, 1, before, sf, rf)]
    for copy in fact_copies:
        copy.start()

    def swap(source, target, i, sends, recvs):
        return [
            pltpu.make_async_remote_copy(
                src_ref=source[n],
                dst_ref=target[n],
                send_sem=sends.at[i, n],
                recv_sem=recvs.at[i, n],
                device_id={"gz": partner},
                device_id_type=MESH,
            )
            for n in range(2)
        ]

    def gathered(i):
        rows = pl.ds(CX * i, CX)
        pieces = [r1.at[chip, rows, :, side], r1.at[1 - chip, rows, :, 1 - side]]
        return swap(pieces, pieces, i, ss2, rs2)

    def to_sibling(source, target, i, send, recv):
        return pltpu.make_async_remote_copy(
            src_ref=source,
            dst_ref=target,
            send_sem=send.at[i],
            recv_sem=recv.at[i],
            device_id={"gz": sibling},
            device_id_type=MESH,
        )

    def quarters(i):
        rows = pl.ds(CX * i, CX)
        away = to_sibling(y1.at[1 - core, rows], r2.at[core, rows], i, ss3, rs3)
        return away, pltpu.make_async_copy(y1.at[core, rows], r2.at[core, rows], ls3.at[i])

    def blocks(i):
        rows = pl.ds(CX * i, CX)
        mine = r3.at[rows, pl.ds(pl.multiple_of(YF * core, YF), YF), :]
        away = to_sibling(zi.at[1 - core, rows], mine, i, ss4, rs4)
        return away, pltpu.make_async_copy(zi.at[core, rows], mine, ls4.at[i])

    def partials(i):
        rows = pl.ds(CX * i, CX)
        pieces = [yp.at[1 - chip, rows, :, side], yp.at[chip, rows, :, 1 - side]]
        return swap(pieces, [yr.at[n, rows] for n in range(2)], i, ss5, rs5)

    @pl.loop(0, CH)
    def _(i):
        whole = r1.at[0, pl.ds(CX * i, CX)]
        pltpu.make_async_copy(whole, whole, rs1.at[i]).wait()
        for copy in gathered(i):
            copy.start()

    for n in range(2, 12):
        fills[n].wait()
    loads[3].wait()

    @pl.loop(0, CH)
    def _(i):
        for copy in gathered(i):
            copy.wait_recv()

        @pl.loop(0, CX)
        def _(k):
            x = CX * i + k
            both = jnp.concatenate(
                [r1[0, x].reshape(NY, LANES), r1[1, x].reshape(NY, LANES)], axis=1
            )
            full = jnp.concatenate([both, turned_pair(both, sign)], axis=0)
            high, low = split(full)
            bh[...] = high
            bl[...] = low
            for q in range(2):
                table = 2 * chip + q
                y1[q, x] = product(fyh[table], fyl[table], bh[...], bl[...])

        away, stay = quarters(i)
        away.start()
        stay.start()
        away.wait_recv()
        stay.wait()

        @pl.loop(0, CX // 2)
        def _(k):
            x = CX * i + 2 * k
            for j in range(2):
                line = jnp.concatenate([r2[0, x + j], r2[1, x + j]], axis=1)
                high, low = split(line)
                ah[j * YF : (j + 1) * YF] = high
                al[j * YF : (j + 1) * YF] = low
            for n in range(2):
                out = product(ah[...], al[...], wzh[n], wzl[n])
                for j in range(2):
                    lines = slice(j * YF, (j + 1) * YF)
                    real, imag = out[lines, :256], out[lines, 256:]
                    g_real = green[0, x + j, :, 256 * n : 256 * n + 256]
                    g_imag = green[1, x + j, :, 256 * n : 256 * n + 256]
                    high, low = split(real * g_real - imag * g_imag)
                    qh[lines, 512 * n : 512 * n + 256] = high
                    ql[lines, 512 * n : 512 * n + 256] = low
                    high, low = split(real * g_imag + imag * g_real)
                    qh[lines, 512 * n + 256 : 512 * n + 512] = high
                    ql[lines, 512 * n + 256 : 512 * n + 512] = low
            out = product(qh[...], ql[...], wih[...], wil[...])
            for j in range(2):
                for d in range(2):
                    zi[d, x + j] = out[j * YF : (j + 1) * YF, d * 256 : (d + 1) * 256]

        away, stay = blocks(i)
        away.start()
        stay.start()
        away.wait_recv()
        stay.wait()

        @pl.loop(0, CX)
        def _(k):
            x = CX * i + k
            both = r3[x]
            full = jnp.concatenate([both, turned_pair(both, sign)], axis=0)
            high, low = split(full)
            bh[...] = high
            bl[...] = low
            out = product(fyih[chip], fyil[chip], bh[...], bl[...])
            for b in range(2):
                yp[b, x] = out[:, b * LANES : (b + 1) * LANES].reshape(4, 2, 32, LANES)

        for copy in partials(i):
            copy.start()

    @pl.loop(0, CH)
    def _(i):
        for copy in partials(i):
            copy.wait_recv()

        @pl.loop(0, CX)
        def _(k):
            x = CX * i + k
            yi[0, x] = yp[chip, x, :, side] + yr[0, x]
            yi[1, x] = yp[1 - chip, x, :, 1 - side] + yr[1, x]

        def part(p):
            group, pair, first = place(p)
            other = jnp.where(pair == side, 0, 1)
            return yi.at[other, pl.ds(CX * i, CX), group, pl.ds(first, ROWS)]

        mine = r4.at[i, pl.ds(CX * me, CX)]

        @pl.loop(1, GY)
        def _(k):
            p = lax.rem(me + k, GY)
            pltpu.make_async_remote_copy(
                src_ref=part(p),
                dst_ref=mine,
                send_sem=ss6.at[i],
                recv_sem=rs6.at[i],
                device_id=across(p),
                device_id_type=MESH,
            ).start()

        pltpu.make_async_copy(part(me), mine, rs6.at[i]).start()

    acc[...] = jnp.zeros_like(acc)

    @pl.loop(0, CH)
    def _(i):
        pltpu.make_async_copy(r4.at[i], r4.at[i], rs6.at[i]).wait()
        lh, ll = fxih[i], fxil[i]
        for k in range(ROWS // 2):
            pair = jnp.concatenate([r4[i, :, 2 * k, :], r4[i, :, 2 * k + 1, :]], axis=1)
            full = jnp.concatenate([pair, turned_pair(pair, sign)], axis=0)
            high, low = split(full)
            acc[k] += product(lh, ll, high, low)

    scale = 1.0 / float(PAD) ** 3

    @pl.loop(0, ROWS // 2)
    def _(k):
        for j in range(2):
            flat = acc[k, :, j * LANES : (j + 1) * LANES].T * scale
            adj[0, 2 * k + j] = src[0, 2 * k + j] - flat[:DEPTH]
            adj[1, 2 * k + j] = src[1, 2 * k + j] - flat[DEPTH:]

    loads[2].wait()
    holds = (mz == 1) | (mz == 2)
    slot = jnp.where(mz == 2, 1, 0)

    def slab_copy(step, turn):
        return pltpu.make_async_remote_copy(
            src_ref=slab,
            dst_ref=slabs.at[1 - step, slot],
            send_sem=sp.at[step + 1, turn],
            recv_sem=rp.at[1 - step, slot],
            device_id={
                "gy": lax.rem(me + GY + step, GY),
                "gz": lax.rem(mz + turn, GZ),
            },
            device_id_type=MESH,
        )

    reaches = [
        (step, turn) for step in (-1, 0, 1) for turn in range(GZ) if step or turn
    ]

    @pl.when(holds)
    def _():
        planes = pl.ds(slab_z, 16)
        field = adj[0, :, planes, :] * fwd[0] - adj[1, :, planes, :] * fwd[1]
        total = jnp.sum(field, axis=1) * (GAP / SLAB)
        slab[...] = total
        slabs[1, slot] = total
        for step, turn in reaches:
            slab_copy(step, turn).start()

    for copy in fact_copies:
        copy.wait()
    for step in range(3):
        for source in range(2):
            arrived = pltpu.make_async_copy(slab, slabs.at[step, source], rp.at[step, source])
            if step == 1:

                @pl.when(mz != source + 1)
                def _(arrived=arrived):
                    arrived.wait()

            else:
                arrived.wait()

    summed = [slabs[step, 0] + slabs[step, 1] for step in range(3)]
    sense = jnp.concatenate(
        [summed[0][ROWS - RADIUS :], summed[1], summed[2][:RADIUS]], axis=0
    )
    weighted = jnp.where(inside, wide(fact) * sense, 0.0)
    scaled = exact(weighted, filt[...]) / jnp.where(inside, weight16, 1.0)
    grad[...] = tent_rows(scaled)

    @pl.when(holds)
    def _():
        for step, turn in reaches:
            slab_copy(step, turn).wait_send()

    @pl.loop(0, CH)
    def _(i):
        sent = s1.at[i, pl.ds(0, CX * (GY - 1))]
        pltpu.make_async_copy(sent, sent, ss1.at[i]).wait()
        for copy in gathered(i) + partials(i):
            copy.wait_send()
        quarters(i)[0].wait_send()
        blocks(i)[0].wait_send()
        pltpu.make_async_copy(sent, sent, ss6.at[i]).wait()


def shards(source, contrast, green, forward_field, density, thresh_index):
    levels = 0.35 + 0.1 * thresh_index.astype(F32)
    threshold = jnp.broadcast_to(
        levels[:, None, :, None], (levels.shape[0], TILE_Y, levels.shape[1], TILE_X)
    ).reshape(ROWS, NX)
    constants = tables()
    anywhere = pl.BlockSpec(memory_space=pl.ANY)
    vmem = pl.BlockSpec(memory_space=pltpu.VMEM)
    dma = pltpu.SemaphoreType.DMA
    block = pltpu.VMEM
    scratch = [
        block((2, ROWS, DEPTH, NX), F32),
        block((ROWS, DEPTH, NX), F32),
        block((2, ROWS, 16, NX), F32),
        block((2, XF, YF, PAD), F32),
    ]
    scratch += [block(table.shape, table.dtype) for table in constants]
    scratch += [
        block((ROWS, 2 * NX, LANES), BF16),
        block((ROWS, 2 * NX, LANES), BF16),
        block((CH, GY * CX, ROWS, LANES), F32),
        block((2, XF, 4, 2, 32, LANES), F32),
        block((2, XF, YF, 2 * LANES), F32),
        block((2, XF, YF, 2 * LANES), F32),
        block((2, XF, YF, 2 * LANES), F32),
        block((XF, 2 * YF, 2 * LANES), F32),
        block((2, XF, 4, 2, 32, LANES), F32),
        block((2, XF, 4, 32, LANES), F32),
        block((2, XF, 4, 32, LANES), F32),
        block((CH, GY * CX, ROWS, LANES), F32),
        block((ROWS // 2, NX, 2 * LANES), F32),
        block((PAD, 2 * LANES), BF16),
        block((PAD, 2 * LANES), BF16),
        block((2 * YF, 2 * NZ), BF16),
        block((2 * YF, 2 * NZ), BF16),
        block((2 * YF, 2 * PAD), BF16),
        block((2 * YF, 2 * PAD), BF16),
        block((3, ROWS, NX), F32),
        block((3, ROWS, NX), F32),
        block((ROWS, NX), F32),
        block((3, 2, ROWS, NX), F32),
        dma((4,)),
        dma((14,)),
    ]
    scratch += [dma((2,)) for _ in range(4)]
    scratch += [dma((3, GZ)), dma((3, 2))]
    scratch += [dma((CH,))] * 2 + [dma((CH, 2))] * 2
    scratch += [dma((CH,))] * 6 + [dma((CH, 2))] * 2 + [dma((CH,))] * 2
    return pl.pallas_call(
        kernel,
        out_shape=(
            jax.ShapeDtypeStruct((2, ROWS, DEPTH, NX), F32),
            jax.ShapeDtypeStruct((ROWS, NX), F32),
            jax.ShapeDtypeStruct((ROWS, NX), F32),
        ),
        in_specs=[anywhere] * 4 + [vmem] * 2 + [anywhere] * 14,
        out_specs=(vmem, vmem, vmem),
        scratch_shapes=scratch,
        compiler_params=pltpu.CompilerParams(
            collective_id=0, has_side_effects=True, vmem_limit_bytes=62 << 20
        ),
    )(source, contrast, forward_field, green, density, threshold, *map(jnp.asarray, constants))


def solution(mesh):
    return jax.shard_map(
        shards,
        mesh=mesh,
        in_specs=(
            P(None, "gy", "gz", None),
            P("gy", "gz", None),
            P(None, "gy", "gz", None),
            P(None, "gy", "gz", None),
            P("gy", None),
            P("gy", None),
        ),
        out_specs=(P(None, "gy", "gz", None), P("gy", None), P("gy", None)),
        check_vma=False,
    )
```

```python
import functools

import jax
import jax.numpy as jnp
import ml_dtypes
import numpy as np
from jax import lax
from jax.experimental import pallas as pl
from jax.experimental.pallas import tpu as pltpu
from jax.sharding import PartitionSpec as P

NX = NY = NZ = 256
PAD = 512
SLAB = 32
RADIUS = 4
TILE_Y = 4
TILE_X = 16
Z0 = 112
SHARP = 8.0
GAP = 11.0

GY = 32
GZ = 4
ROWS = NY // GY
DEPTH = NZ // GZ
XF = PAD // GY
YF = PAD // GZ
LANES = 2 * DEPTH
CH = 8
CX = XF // CH
LAST = 6
JOIN = CH // 4

F32 = jnp.float32
BF16 = jnp.bfloat16
MESH = pl.DeviceIdType.MESH


def halves(table):
    high = table.astype(ml_dtypes.bfloat16)
    low = (table - high.astype(np.float64)).astype(ml_dtypes.bfloat16)
    return high, low


def tables():
    k = np.arange(PAD)[:, None]
    p = np.arange(NX)[None, :]
    angle = (k * p % PAD) * (2.0 * np.pi / PAD)
    cos, sin = np.cos(angle), np.sin(angle)
    order = np.arange(PAD).reshape(GY, CH, CX).transpose(1, 0, 2).reshape(CH, GY * CX)
    fx = np.concatenate([cos[order], sin[order]], axis=2)
    joined = order.reshape(CH // JOIN, JOIN * GY * CX)
    fy = np.concatenate([cos, sin], axis=1).reshape(GZ, YF, 2 * NY)
    half = (2, PAD // 2, NY)
    fyi = np.concatenate(
        [cos.reshape(half).transpose(0, 2, 1), -sin.reshape(half).transpose(0, 2, 1)],
        axis=2,
    )
    fxi = np.concatenate(
        [cos[joined].transpose(0, 2, 1), -sin[joined].transpose(0, 2, 1)], axis=2
    )
    shape = (2, 256, 2, 2, DEPTH)
    ct = cos.reshape(shape).transpose(0, 3, 2, 4, 1)
    st = sin.reshape(shape).transpose(0, 3, 2, 4, 1)
    re_rows = np.concatenate([ct, -st], axis=4)
    im_rows = np.concatenate([st, ct], axis=4)
    wz = np.stack([re_rows, im_rows], axis=3).reshape(2, 2 * NZ, 512)
    wzi = wz.transpose(0, 2, 1).reshape(1024, 512)
    flat = []
    for table in (fx, fy, fyi, fxi, wz, wzi):
        flat.extend(halves(table))
    cells = np.arange(NX)
    tent = np.maximum(RADIUS + 1 - np.abs(cells[:, None] - cells[None, :]), 0).astype(
        np.float32
    )
    filt = tent / tent.sum(axis=1, keepdims=True)
    return flat + [filt, np.ascontiguousarray(filt.T)]


def split(value):
    high = value.astype(BF16)
    return high, (value - high.astype(F32)).astype(BF16)


def product(ah, al, bh, bl):
    dot = functools.partial(jnp.dot, preferred_element_type=F32)
    return dot(ah, bh) + dot(al, bh) + dot(ah, bl)


def turned(block, sign):
    return pltpu.roll(block, DEPTH, 1) * sign


def turned_pair(pair, sign):
    return jnp.concatenate(
        [turned(pair[:, :LANES], sign), turned(pair[:, LANES:], sign)], axis=1
    )


def kernel(*refs):
    (src_h, con_h, fwd_h, green_h, dens, level) = refs[:6]
    tabs_h = refs[6:20]
    adj, proj, grad = refs[20:23]
    (src, con, fwd, green) = refs[23:27]
    tabs = refs[27:41]
    (sth, stl, s1, r1, y1, r2, zi, r3, yp, yr, yi, r4, acc) = refs[41:54]
    (bh, bl, ah, al, qh, ql, near, fact, slab, slabs) = refs[54:64]
    (in_sem, tab_sem, sn, rn, sf, rf, sp, rp) = refs[64:72]
    (ss1, rs1, ss2, rs2, ss3, rs3, ls3, ss4, rs4, ls4, ss5, rs5, ss6, rs6) = refs[72:86]
    fxh, fxl, fyh, fyl, fyih, fyil, fxih, fxil, wzh, wzl, wih, wil, filt, filt_t = tabs

    me = lax.axis_index("gy")
    mz = lax.axis_index("gz")
    after, before = lax.rem(me + 1, GY), lax.rem(me + GY - 1, GY)
    core, chip = lax.rem(mz, 2), mz // 2
    side = lax.rem(me // 4, 2)
    sibling = mz + 1 - 2 * core
    partner = lax.rem(mz + 2, GZ)

    def place(p):
        return p // 8, lax.rem(p // 4, 2), pl.multiple_of(ROWS * lax.rem(p, 4), ROWS)

    def across(p):
        same = lax.rem(p // 4, 2) == side
        return {"gy": p, "gz": jnp.where(same, mz, partner)}

    slab_z = pl.multiple_of(jnp.where(mz == 1, 48, 0), 16)
    loads = [
        pltpu.make_async_copy(src_h, src, in_sem.at[0]),
        pltpu.make_async_copy(con_h, con, in_sem.at[1]),
        pltpu.make_async_copy(fwd_h.at[:, :, pl.ds(slab_z, 16), :], fwd, in_sem.at[2]),
        pltpu.make_async_copy(green_h, green, in_sem.at[3]),
    ]
    fills = [
        pltpu.make_async_copy(tabs_h[n], tabs[n], tab_sem.at[n]) for n in range(14)
    ]
    for copy in (loads[0], loads[1], fills[0], fills[1]):
        copy.start()

    barrier = pltpu.get_barrier_semaphore()

    @pl.loop(1, GY)
    def _(k):
        pl.semaphore_signal(
            barrier, inc=1, device_id=across(lax.rem(me + k, GY)), device_id_type=MESH
        )

    for k in range(GZ):
        other = lax.rem(mz + k, GZ)
        for row in (after, before) + ((me,) if k else ()):
            pl.semaphore_signal(
                barrier,
                inc=1,
                device_id={"gy": row, "gz": other},
                device_id_type=MESH,
            )

    lane = lax.broadcasted_iota(jnp.int32, (1, LANES), 1)
    sign = jnp.where(lane < DEPTH, 1.0, -1.0).astype(F32)

    loads[0].wait()
    loads[1].wait()
    for copy in fills[12:] + fills[2:6] + fills[8:12] + loads[3:] + fills[6:8] + loads[2:3]:
        copy.start()

    @pl.loop(0, ROWS)
    def _(y):
        weight = con[y]
        both = jnp.concatenate([src[0, y] * weight, src[1, y] * weight], axis=0)
        flat = both.T
        full = jnp.concatenate([flat, turned(flat, sign)], axis=0)
        high, low = split(full)
        sth[y] = high
        stl[y] = low

    fills[0].wait()
    fills[1].wait()

    pl.semaphore_wait(barrier, (GY - 1) + 2 * GZ + (GZ - 1))

    def near_copy(buffer, slot, target, sems, recv):
        return pltpu.make_async_remote_copy(
            src_ref=buffer.at[2],
            dst_ref=buffer.at[slot],
            send_sem=sems.at[slot],
            recv_sem=recv.at[slot],
            device_id={"gy": target},
            device_id_type=MESH,
        )

    near[2] = dens[...]
    near_copies = [near_copy(near, 0, after, sn, rn), near_copy(near, 1, before, sn, rn)]
    for copy in near_copies:
        copy.start()

    def forward_x(i):
        lh, ll = fxh[i], fxl[i]
        for k in range(ROWS // 2):
            rh = jnp.concatenate([sth[2 * k], sth[2 * k + 1]], axis=1)
            rl = jnp.concatenate([stl[2 * k], stl[2 * k + 1]], axis=1)
            out = product(lh, ll, rh, rl)
            s1[i, :, 2 * k, :] = out[:, :LANES]
            s1[i, :, 2 * k + 1, :] = out[:, LANES:]

        def part(p):
            return s1.at[i, pl.ds(CX * p, CX)]

        group, pair, first = place(me)
        mine = r1.at[chip, pl.ds(CX * i, CX), group, pair, pl.ds(first, ROWS)]

        @pl.loop(1, GY)
        def _(k):
            p = lax.rem(me + k, GY)
            pltpu.make_async_remote_copy(
                src_ref=part(p),
                dst_ref=mine,
                send_sem=ss1.at[i],
                recv_sem=rs1.at[i],
                device_id=across(p),
                device_id_type=MESH,
            ).start()

        pltpu.make_async_copy(part(me), mine, rs1.at[i]).start()

    def wide(buffer):
        rows = jnp.concatenate(
            [buffer[0][ROWS - RADIUS :], buffer[2], buffer[1][:RADIUS]], axis=0
        )
        return jnp.where(inside, rows, 0.0)

    row = ROWS * me - RADIUS + lax.broadcasted_iota(jnp.int32, (2 * ROWS, NX), 0)
    inside = (row >= 0) & (row < NY)
    weight16 = jnp.zeros((2 * ROWS, NX), F32)
    for offset in range(-RADIUS, RADIUS + 1):
        valid = (row + offset >= 0) & (row + offset < NY)
        weight16 = weight16 + jnp.where(valid, float(RADIUS + 1 - abs(offset)), 0.0)

    def tent_rows(rows):
        total = jnp.zeros((ROWS, NX), F32)
        for offset in range(-RADIUS, RADIUS + 1):
            start = RADIUS + offset
            total = total + float(RADIUS + 1 - abs(offset)) * rows[start : start + ROWS]
        return total

    exact = functools.partial(
        jnp.dot, preferred_element_type=F32, precision=lax.Precision.HIGHEST
    )
    fact_copies = [near_copy(fact, 0, after, sf, rf), near_copy(fact, 1, before, sf, rf)]

    def project():
        fills[12].wait()
        fills[13].wait()
        for copy in near_copies:
            copy.wait()
        smooth = tent_rows(wide(near)) / weight16[RADIUS : RADIUS + ROWS]
        filtered = exact(smooth, filt_t[...])
        threshold = level[...]
        steep = jnp.tanh(SHARP * (filtered - threshold))
        shift = jnp.tanh(SHARP * threshold)
        below = shift + jnp.tanh(SHARP * (1.0 - threshold))
        proj[...] = (shift + steep) / below
        fact[2] = SHARP * (1.0 - steep * steep) / below
        for copy in fact_copies:
            copy.start()

    def swap(source, target, i, sends, recvs):
        return [
            pltpu.make_async_remote_copy(
                src_ref=source[n],
                dst_ref=target[n],
                send_sem=sends.at[i, n],
                recv_sem=recvs.at[i, n],
                device_id={"gz": partner},
                device_id_type=MESH,
            )
            for n in range(2)
        ]

    def gathered(i):
        rows = pl.ds(CX * i, CX)
        pieces = [r1.at[chip, rows, :, side], r1.at[1 - chip, rows, :, 1 - side]]
        return swap(pieces, pieces, i, ss2, rs2)

    def to_sibling(source, target, i, send, recv):
        return pltpu.make_async_remote_copy(
            src_ref=source,
            dst_ref=target,
            send_sem=send.at[i],
            recv_sem=recv.at[i],
            device_id={"gz": sibling},
            device_id_type=MESH,
        )

    def quarters(i):
        rows = pl.ds(CX * i, CX)
        away = to_sibling(y1.at[1 - core, rows], r2.at[core, rows], i, ss3, rs3)
        return away, pltpu.make_async_copy(y1.at[core, rows], r2.at[core, rows], ls3.at[i])

    def blocks(i):
        rows = pl.ds(CX * i, CX)
        mine = r3.at[rows, pl.ds(pl.multiple_of(YF * core, YF), YF), :]
        away = to_sibling(zi.at[1 - core, rows], mine, i, ss4, rs4)
        return away, pltpu.make_async_copy(zi.at[core, rows], mine, ls4.at[i])

    def partials(i):
        rows = pl.ds(CX * i, CX)
        pieces = [yp.at[1 - chip, rows, :, side], yp.at[chip, rows, :, 1 - side]]
        return swap(pieces, [yr.at[n, rows] for n in range(2)], i, ss5, rs5)

    def gather(i):
        whole = r1.at[0, pl.ds(CX * i, CX)]
        pltpu.make_async_copy(whole, whole, rs1.at[i]).wait()
        for copy in gathered(i):
            copy.start()

    def forward_y(i):
        for copy in gathered(i):
            copy.wait_recv()

        @pl.loop(0, CX)
        def _(k):
            x = CX * i + k
            both = jnp.concatenate(
                [r1[0, x].reshape(NY, LANES), r1[1, x].reshape(NY, LANES)], axis=1
            )
            full = jnp.concatenate([both, turned_pair(both, sign)], axis=0)
            high, low = split(full)
            bh[...] = high
            bl[...] = low
            for q in range(2):
                table = 2 * chip + q
                y1[q, x] = product(fyh[table], fyl[table], bh[...], bl[...])

        away, stay = quarters(i)
        away.start()
        stay.start()

    def along_z(i):
        away, stay = quarters(i)
        away.wait_recv()
        stay.wait()

        @pl.loop(0, CX // 2)
        def _(k):
            x = CX * i + 2 * k
            for j in range(2):
                line = jnp.concatenate([r2[0, x + j], r2[1, x + j]], axis=1)
                high, low = split(line)
                ah[j * YF : (j + 1) * YF] = high
                al[j * YF : (j + 1) * YF] = low
            for n in range(2):
                out = product(ah[...], al[...], wzh[n], wzl[n])
                for j in range(2):
                    lines = slice(j * YF, (j + 1) * YF)
                    real, imag = out[lines, :256], out[lines, 256:]
                    g_real = green[0, x + j, :, 256 * n : 256 * n + 256]
                    g_imag = green[1, x + j, :, 256 * n : 256 * n + 256]
                    high, low = split(real * g_real - imag * g_imag)
                    qh[lines, 512 * n : 512 * n + 256] = high
                    ql[lines, 512 * n : 512 * n + 256] = low
                    high, low = split(real * g_imag + imag * g_real)
                    qh[lines, 512 * n + 256 : 512 * n + 512] = high
                    ql[lines, 512 * n + 256 : 512 * n + 512] = low
            out = product(qh[...], ql[...], wih[...], wil[...])
            for j in range(2):
                for d in range(2):
                    zi[d, x + j] = out[j * YF : (j + 1) * YF, d * 256 : (d + 1) * 256]

        away, stay = blocks(i)
        away.start()
        stay.start()

    def inverse_y(i):
        away, stay = blocks(i)
        away.wait_recv()
        stay.wait()

        @pl.loop(0, CX)
        def _(k):
            x = CX * i + k
            both = r3[x]
            full = jnp.concatenate([both, turned_pair(both, sign)], axis=0)
            high, low = split(full)
            bh[...] = high
            bl[...] = low
            out = product(fyih[chip], fyil[chip], bh[...], bl[...])
            for b in range(2):
                yp[b, x] = out[:, b * LANES : (b + 1) * LANES].reshape(4, 2, 32, LANES)

        for copy in partials(i):
            copy.start()

    def add_halves(i):
        for copy in partials(i):
            copy.wait_recv()

        @pl.loop(0, CX)
        def _(k):
            x = CX * i + k
            yi[0, x] = yp[chip, x, :, side] + yr[0, x]
            yi[1, x] = yp[1 - chip, x, :, 1 - side] + yr[1, x]

        def part(p):
            group, pair, first = place(p)
            other = jnp.where(pair == side, 0, 1)
            return yi.at[other, pl.ds(CX * i, CX), group, pl.ds(first, ROWS)]

        mine = r4.at[i, pl.ds(CX * me, CX)]

        @pl.loop(1, GY)
        def _(k):
            p = lax.rem(me + k, GY)
            pltpu.make_async_remote_copy(
                src_ref=part(p),
                dst_ref=mine,
                send_sem=ss6.at[i],
                recv_sem=rs6.at[i],
                device_id=across(p),
                device_id_type=MESH,
            ).start()

        pltpu.make_async_copy(part(me), mine, rs6.at[i]).start()

    def inverse_x(last):
        j = last // JOIN
        for n in range(JOIN):
            whole = r4.at[JOIN * j + n]
            pltpu.make_async_copy(whole, whole, rs6.at[JOIN * j + n]).wait()
        lh, ll = fxih[j], fxil[j]

        def lines(y):
            return jnp.concatenate([r4[JOIN * j + n, :, y, :] for n in range(JOIN)], axis=0)

        for k in range(ROWS // 2):
            pair = jnp.concatenate([lines(2 * k), lines(2 * k + 1)], axis=1)
            full = jnp.concatenate([pair, turned_pair(pair, sign)], axis=0)
            high, low = split(full)
            acc[k] += product(lh, ll, high, low)

    def join_x(i):
        @pl.when(lax.rem(i, JOIN) == JOIN - 1)
        def _():
            inverse_x(i)

    acc[...] = jnp.zeros_like(acc)

    @pl.loop(0, CH + LAST)
    def _(step):
        def stage(lag, work):
            i = step - lag

            @pl.when((i >= 0) & (i < CH))
            def _():
                work(i)

        stage(0, forward_x)

        @pl.when(step == 1)
        def _():
            for n in range(2, 12):
                fills[n].wait()
            loads[3].wait()

        stage(1, gather)
        stage(4, inverse_y)
        stage(3, along_z)
        stage(5, add_halves)
        stage(2, forward_y)
        stage(LAST, join_x)

        @pl.when(step == 2)
        def _():
            project()

    scale = 1.0 / float(PAD) ** 3

    @pl.loop(0, ROWS // 2)
    def _(k):
        for j in range(2):
            flat = acc[k, :, j * LANES : (j + 1) * LANES].T * scale
            adj[0, 2 * k + j] = src[0, 2 * k + j] - flat[:DEPTH]
            adj[1, 2 * k + j] = src[1, 2 * k + j] - flat[DEPTH:]

    loads[2].wait()
    holds = (mz == 1) | (mz == 2)
    slot = jnp.where(mz == 2, 1, 0)

    def slab_copy(step, turn):
        return pltpu.make_async_remote_copy(
            src_ref=slab,
            dst_ref=slabs.at[1 - step, slot],
            send_sem=sp.at[step + 1, turn],
            recv_sem=rp.at[1 - step, slot],
            device_id={
                "gy": lax.rem(me + GY + step, GY),
                "gz": lax.rem(mz + turn, GZ),
            },
            device_id_type=MESH,
        )

    reaches = [
        (step, turn) for step in (-1, 0, 1) for turn in range(GZ) if step or turn
    ]

    @pl.when(holds)
    def _():
        planes = pl.ds(slab_z, 16)
        field = adj[0, :, planes, :] * fwd[0] - adj[1, :, planes, :] * fwd[1]
        total = jnp.sum(field, axis=1) * (GAP / SLAB)
        slab[...] = total
        slabs[1, slot] = total
        for step, turn in reaches:
            slab_copy(step, turn).start()

    for copy in fact_copies:
        copy.wait()
    for step in range(3):
        for source in range(2):
            arrived = pltpu.make_async_copy(slab, slabs.at[step, source], rp.at[step, source])
            if step == 1:

                @pl.when(mz != source + 1)
                def _(arrived=arrived):
                    arrived.wait()

            else:
                arrived.wait()

    summed = [slabs[step, 0] + slabs[step, 1] for step in range(3)]
    sense = jnp.concatenate(
        [summed[0][ROWS - RADIUS :], summed[1], summed[2][:RADIUS]], axis=0
    )
    weighted = jnp.where(inside, wide(fact) * sense, 0.0)
    scaled = exact(weighted, filt[...]) / jnp.where(inside, weight16, 1.0)
    grad[...] = tent_rows(scaled)

    @pl.when(holds)
    def _():
        for step, turn in reaches:
            slab_copy(step, turn).wait_send()

    @pl.loop(0, CH)
    def _(i):
        sent = s1.at[i, pl.ds(0, CX * (GY - 1))]
        pltpu.make_async_copy(sent, sent, ss1.at[i]).wait()
        for copy in gathered(i) + partials(i):
            copy.wait_send()
        quarters(i)[0].wait_send()
        blocks(i)[0].wait_send()
        pltpu.make_async_copy(sent, sent, ss6.at[i]).wait()


def shards(source, contrast, green, forward_field, density, thresh_index):
    levels = 0.35 + 0.1 * thresh_index.astype(F32)
    threshold = jnp.broadcast_to(
        levels[:, None, :, None], (levels.shape[0], TILE_Y, levels.shape[1], TILE_X)
    ).reshape(ROWS, NX)
    constants = tables()
    anywhere = pl.BlockSpec(memory_space=pl.ANY)
    vmem = pl.BlockSpec(memory_space=pltpu.VMEM)
    dma = pltpu.SemaphoreType.DMA
    block = pltpu.VMEM
    scratch = [
        block((2, ROWS, DEPTH, NX), F32),
        block((ROWS, DEPTH, NX), F32),
        block((2, ROWS, 16, NX), F32),
        block((2, XF, YF, PAD), F32),
    ]
    scratch += [block(table.shape, table.dtype) for table in constants]
    scratch += [
        block((ROWS, 2 * NX, LANES), BF16),
        block((ROWS, 2 * NX, LANES), BF16),
        block((CH, GY * CX, ROWS, LANES), F32),
        block((2, XF, 4, 2, 32, LANES), F32),
        block((2, XF, YF, 2 * LANES), F32),
        block((2, XF, YF, 2 * LANES), F32),
        block((2, XF, YF, 2 * LANES), F32),
        block((XF, 2 * YF, 2 * LANES), F32),
        block((2, XF, 4, 2, 32, LANES), F32),
        block((2, XF, 4, 32, LANES), F32),
        block((2, XF, 4, 32, LANES), F32),
        block((CH, GY * CX, ROWS, LANES), F32),
        block((ROWS // 2, NX, 2 * LANES), F32),
        block((PAD, 2 * LANES), BF16),
        block((PAD, 2 * LANES), BF16),
        block((2 * YF, 2 * NZ), BF16),
        block((2 * YF, 2 * NZ), BF16),
        block((2 * YF, 2 * PAD), BF16),
        block((2 * YF, 2 * PAD), BF16),
        block((3, ROWS, NX), F32),
        block((3, ROWS, NX), F32),
        block((ROWS, NX), F32),
        block((3, 2, ROWS, NX), F32),
        dma((4,)),
        dma((14,)),
    ]
    scratch += [dma((2,)) for _ in range(4)]
    scratch += [dma((3, GZ)), dma((3, 2))]
    scratch += [dma((CH,))] * 2 + [dma((CH, 2))] * 2
    scratch += [dma((CH,))] * 6 + [dma((CH, 2))] * 2 + [dma((CH,))] * 2
    return pl.pallas_call(
        kernel,
        out_shape=(
            jax.ShapeDtypeStruct((2, ROWS, DEPTH, NX), F32),
            jax.ShapeDtypeStruct((ROWS, NX), F32),
            jax.ShapeDtypeStruct((ROWS, NX), F32),
        ),
        in_specs=[anywhere] * 4 + [vmem] * 2 + [anywhere] * 14,
        out_specs=(vmem, vmem, vmem),
        scratch_shapes=scratch,
        compiler_params=pltpu.CompilerParams(
            collective_id=0, has_side_effects=True, vmem_limit_bytes=62 << 20
        ),
    )(source, contrast, forward_field, green, density, threshold, *map(jnp.asarray, constants))


def solution(mesh):
    return jax.shard_map(
        shards,
        mesh=mesh,
        in_specs=(
            P(None, "gy", "gz", None),
            P("gy", "gz", None),
            P(None, "gy", "gz", None),
            P(None, "gy", "gz", None),
            P("gy", None),
            P("gy", None),
        ),
        out_specs=(P(None, "gy", "gz", None), P("gy", None), P("gy", None)),
        check_vma=False,
    )
```

```python
import functools

import jax
import jax.numpy as jnp
import ml_dtypes
import numpy as np
from jax import lax
from jax.experimental import pallas as pl
from jax.experimental.pallas import tpu as pltpu
from jax.sharding import PartitionSpec as P

NX = NY = NZ = 256
PAD = 512
SLAB = 32
RADIUS = 4
TILE_Y = 4
TILE_X = 16
Z0 = 112
SHARP = 8.0
GAP = 11.0

GY = 32
GZ = 4
ROWS = NY // GY
DEPTH = NZ // GZ
XF = PAD // GY
YF = PAD // GZ
LANES = 2 * DEPTH
CH = 8
CX = XF // CH
EXTRA = 4
BOTH = ROWS + EXTRA
EARLY = 2
LAST = 6
JOIN = CH // 4

F32 = jnp.float32
BF16 = jnp.bfloat16
MESH = pl.DeviceIdType.MESH


def halves(table):
    high = table.astype(ml_dtypes.bfloat16)
    low = (table - high.astype(np.float64)).astype(ml_dtypes.bfloat16)
    return high, low


def tables():
    k = np.arange(PAD)[:, None]
    p = np.arange(NX)[None, :]
    angle = (k * p % PAD) * (2.0 * np.pi / PAD)
    cos, sin = np.cos(angle), np.sin(angle)
    order = np.arange(PAD).reshape(GY, CH, CX).transpose(1, 0, 2).reshape(CH, GY * CX)
    fx = np.concatenate([cos[order], sin[order]], axis=2)
    joined = order.reshape(CH // JOIN, JOIN * GY * CX)
    by_pair = np.arange(NY).reshape(4, 2, 32).transpose(1, 0, 2).reshape(NY)
    fy = np.concatenate([cos[:, by_pair], sin[:, by_pair]], axis=1)
    fy = fy.reshape(GZ, YF, 2 * NY)
    half = (2, PAD // 2, NY)
    fyi = np.concatenate(
        [cos.reshape(half).transpose(0, 2, 1), -sin.reshape(half).transpose(0, 2, 1)],
        axis=2,
    )
    fxi = np.concatenate(
        [cos[joined].transpose(0, 2, 1), -sin[joined].transpose(0, 2, 1)], axis=2
    )
    shape = (2, 256, 2, 2, DEPTH)
    ct = cos.reshape(shape).transpose(0, 3, 2, 4, 1)
    st = sin.reshape(shape).transpose(0, 3, 2, 4, 1)
    re_rows = np.concatenate([ct, -st], axis=4)
    im_rows = np.concatenate([st, ct], axis=4)
    wz = np.stack([re_rows, im_rows], axis=3).reshape(2, 2 * NZ, 512)
    wzi = wz.transpose(0, 2, 1).reshape(1024, 2, 256).transpose(1, 0, 2)
    flat = []
    for table in (fx, fy, fyi, fxi, wz, wzi):
        flat.extend(halves(table))
    cells = np.arange(NX)
    tent = np.maximum(RADIUS + 1 - np.abs(cells[:, None] - cells[None, :]), 0).astype(
        np.float32
    )
    filt = tent / tent.sum(axis=1, keepdims=True)
    return flat + [filt, np.ascontiguousarray(filt.T)]


def split(value):
    high = value.astype(BF16)
    return high, (value - high.astype(F32)).astype(BF16)


def product(ah, al, bh, bl):
    dot = functools.partial(jnp.dot, preferred_element_type=F32)
    return dot(ah, bh) + dot(al, bh) + dot(ah, bl)


def turned(block, sign):
    return pltpu.roll(block, DEPTH, 1) * sign


def turned_pair(pair, sign):
    return jnp.concatenate(
        [turned(pair[:, :LANES], sign), turned(pair[:, LANES:], sign)], axis=1
    )


def kernel(*refs):
    (src_h, con_h, fwd_h, green_h, dens, level) = refs[:6]
    tabs_h = refs[6:20]
    adj, proj, grad = refs[20:23]
    (src, con, fwd, green) = refs[23:27]
    tabs = refs[27:41]
    (sth, stl, s1, r1, y1, r2, zi, r3, yp, yr, yi, r4, acc) = refs[41:54]
    (raw, sw, rw) = refs[86:89]
    (bh, bl, ah, al, qh, ql, near, fact, slab, slabs) = refs[54:64]
    (in_sem, tab_sem, sn, rn, sf, rf, sp, rp) = refs[64:72]
    (ss1, rs1, ss2, rs2, ss3, rs3, _, ss4, rs4, _, ss5, rs5, ss6, rs6) = refs[72:86]
    fxh, fxl, fyh, fyl, fyih, fyil, fxih, fxil, wzh, wzl, wih, wil, filt, filt_t = tabs

    me = lax.axis_index("gy")
    mz = lax.axis_index("gz")
    after, before = lax.rem(me + 1, GY), lax.rem(me + GY - 1, GY)
    core, chip = lax.rem(mz, 2), mz // 2
    side = lax.rem(me // 4, 2)
    sibling = mz + 1 - 2 * core
    partner = lax.rem(mz + 2, GZ)

    def place(p):
        return p // 8, lax.rem(p // 4, 2), lax.rem(p, 4)

    def across(p):
        same = lax.rem(p // 4, 2) == side
        return {"gy": p, "gz": jnp.where(same, mz, partner)}

    slab_z = pl.multiple_of(jnp.where(mz == 1, 48, 0), 16)
    loads = [
        pltpu.make_async_copy(src_h, src, in_sem.at[0]),
        pltpu.make_async_copy(con_h, con, in_sem.at[1]),
        pltpu.make_async_copy(fwd_h.at[:, :, pl.ds(slab_z, 16), :], fwd, in_sem.at[2]),
        pltpu.make_async_copy(green_h, green, in_sem.at[3]),
    ]
    fills = [
        pltpu.make_async_copy(tabs_h[n], tabs[n], tab_sem.at[n]) for n in range(14)
    ]
    for copy in (loads[0], loads[1], fills[0], fills[1]):
        copy.start()

    barrier = pltpu.get_barrier_semaphore()

    @pl.loop(1, GY)
    def _(k):
        pl.semaphore_signal(
            barrier, inc=1, device_id=across(lax.rem(me + k, GY)), device_id_type=MESH
        )

    for k in range(GZ):
        other = lax.rem(mz + k, GZ)
        for row in (after, before) + ((me,) if k else ()):
            pl.semaphore_signal(
                barrier,
                inc=1,
                device_id={"gy": row, "gz": other},
                device_id_type=MESH,
            )

    lane = lax.broadcasted_iota(jnp.int32, (1, LANES), 1)
    sign = jnp.where(lane < DEPTH, 1.0, -1.0).astype(F32)

    loads[0].wait()
    loads[1].wait()
    for copy in fills[12:] + fills[2:6] + fills[8:12] + loads[3:] + fills[6:8] + loads[2:3]:
        copy.start()

    def stimulus(y):
        weight = con[y]
        both = jnp.concatenate([src[0, y] * weight, src[1, y] * weight], axis=0)
        return both.T

    def keep(y, flat):
        full = jnp.concatenate([flat, turned(flat, sign)], axis=0)
        high, low = split(full)
        sth[y] = high
        stl[y] = low

    @pl.loop(0, EXTRA)
    def _(y):
        raw[0, y] = stimulus(y)

    pl.semaphore_wait(barrier, (GY - 1) + 2 * GZ + (GZ - 1))

    shared = pltpu.make_async_remote_copy(
        src_ref=raw.at[0],
        dst_ref=raw.at[1],
        send_sem=sw,
        recv_sem=rw,
        device_id={"gz": partner},
        device_id_type=MESH,
    )
    shared.start()

    @pl.loop(0, EXTRA)
    def _(y):
        keep(y, raw[0, y])

    @pl.loop(EXTRA, ROWS)
    def _(y):
        keep(y, stimulus(y))

    fills[0].wait()
    fills[1].wait()

    def near_copy(buffer, slot, target, sems, recv):
        return pltpu.make_async_remote_copy(
            src_ref=buffer.at[2],
            dst_ref=buffer.at[slot],
            send_sem=sems.at[slot],
            recv_sem=recv.at[slot],
            device_id={"gy": target},
            device_id_type=MESH,
        )

    near[2] = dens[...]
    near_copies = [near_copy(near, 0, after, sn, rn), near_copy(near, 1, before, sn, rn)]
    for copy in near_copies:
        copy.start()

    def take_shared():
        shared.wait()

        @pl.loop(0, EXTRA)
        def _(y):
            keep(ROWS + y, raw[1, y])

    def by_extra(i, work):
        @pl.when(i < EARLY)
        def _():
            work(i, 0)

        @pl.when(i >= EARLY)
        def _():
            work(i, EXTRA)

    def forward_x(i):
        def rows(k):
            rh = jnp.concatenate([sth[2 * k], sth[2 * k + 1]], axis=1)
            rl = jnp.concatenate([stl[2 * k], stl[2 * k + 1]], axis=1)
            out = product(fxh[i], fxl[i], rh, rl)
            s1[i, :, 2 * k, :] = out[:, :LANES]
            s1[i, :, 2 * k + 1, :] = out[:, LANES:]

        for k in range(ROWS // 2):
            rows(k)

        @pl.when(i >= EARLY)
        def _():
            for k in range(ROWS // 2, BOTH // 2):
                rows(k)

        by_extra(i, spread_x)

    def spread_x(i, extra):
        count = pl.ds(0, ROWS + extra)

        def part(p):
            return s1.at[i, pl.ds(CX * p, CX), count]

        group, pair, rank = place(me)
        mine = r1.at[pl.ds(CX * i, CX), group, pair, rank, count]

        @pl.loop(1, GY)
        def _(k):
            p = lax.rem(me + k, GY)
            pltpu.make_async_remote_copy(
                src_ref=part(p),
                dst_ref=mine,
                send_sem=ss1.at[i],
                recv_sem=rs1.at[i],
                device_id=across(p),
                device_id_type=MESH,
            ).start()

        pltpu.make_async_copy(part(me), mine, rs1.at[i]).start()

    def wide(buffer):
        rows = jnp.concatenate(
            [buffer[0][ROWS - RADIUS :], buffer[2], buffer[1][:RADIUS]], axis=0
        )
        return jnp.where(inside, rows, 0.0)

    row = ROWS * me - RADIUS + lax.broadcasted_iota(jnp.int32, (2 * ROWS, NX), 0)
    inside = (row >= 0) & (row < NY)
    weight16 = jnp.zeros((2 * ROWS, NX), F32)
    for offset in range(-RADIUS, RADIUS + 1):
        valid = (row + offset >= 0) & (row + offset < NY)
        weight16 = weight16 + jnp.where(valid, float(RADIUS + 1 - abs(offset)), 0.0)

    def tent_rows(rows):
        total = jnp.zeros((ROWS, NX), F32)
        for offset in range(-RADIUS, RADIUS + 1):
            start = RADIUS + offset
            total = total + float(RADIUS + 1 - abs(offset)) * rows[start : start + ROWS]
        return total

    exact = functools.partial(
        jnp.dot, preferred_element_type=F32, precision=lax.Precision.HIGHEST
    )
    fact_copies = [near_copy(fact, 0, after, sf, rf), near_copy(fact, 1, before, sf, rf)]

    def project():
        fills[12].wait()
        fills[13].wait()
        for copy in near_copies:
            copy.wait()
        smooth = tent_rows(wide(near)) / weight16[RADIUS : RADIUS + ROWS]
        filtered = exact(smooth, filt_t[...])
        levels = 0.35 + 0.1 * level[...].astype(F32)
        tile = lax.broadcasted_iota(jnp.int32, (2, NX), 1) // TILE_X
        wide_levels = jnp.zeros((2, NX), F32)
        for n in range(NX // TILE_X):
            wide_levels = jnp.where(tile == n, levels[:, n : n + 1], wide_levels)
        upper = lax.broadcasted_iota(jnp.int32, (ROWS, NX), 0) < TILE_Y
        threshold = jnp.where(upper, wide_levels[0:1], wide_levels[1:2])
        steep = jnp.tanh(SHARP * (filtered - threshold))
        shift = jnp.tanh(SHARP * threshold)
        below = shift + jnp.tanh(SHARP * (1.0 - threshold))
        proj[...] = (shift + steep) / below
        fact[2] = SHARP * (1.0 - steep * steep) / below
        for copy in fact_copies:
            copy.start()

    def gathered(i, extra):
        lines = r1.at[pl.ds(CX * i, CX)]
        return pltpu.make_async_remote_copy(
            src_ref=lines.at[:, :, :, :, pl.ds(extra, ROWS - extra)],
            dst_ref=lines.at[:, :, :, :, pl.ds(ROWS + extra, ROWS - extra)],
            send_sem=ss2.at[i],
            recv_sem=rs2.at[i],
            device_id={"gz": partner},
            device_id_type=MESH,
        )

    def to_sibling(source, target, i, send, recv):
        return pltpu.make_async_remote_copy(
            src_ref=source,
            dst_ref=target,
            send_sem=send.at[i],
            recv_sem=recv.at[i],
            device_id={"gz": sibling},
            device_id_type=MESH,
        )

    def quarters(i):
        rows = pl.ds(CX * i, CX)
        return to_sibling(y1.at[rows], r2.at[core, rows], i, ss3, rs3)

    def blocks(i):
        rows = pl.ds(CX * i, CX)
        mine = r3.at[rows, pl.ds(pl.multiple_of(YF * core, YF), YF), :]
        return to_sibling(zi.at[rows], mine, i, ss4, rs4)

    def partials(i):
        rows = pl.ds(CX * i, CX)
        pieces = [yp.at[1 - chip, rows, :, side], yp.at[chip, rows, :, 1 - side]]
        return [
            pltpu.make_async_remote_copy(
                src_ref=pieces[n],
                dst_ref=yr.at[n, rows],
                send_sem=ss5.at[i, n],
                recv_sem=rs5.at[i, n],
                device_id={"gz": partner},
                device_id_type=MESH,
            )
            for n in range(2)
        ]

    def gather(i):
        def pass_on(i, extra):
            whole = r1.at[pl.ds(CX * i, CX), :, :, :, pl.ds(0, ROWS + extra)]
            pltpu.make_async_copy(whole, whole, rs1.at[i]).wait()
            gathered(i, extra).start()

        by_extra(i, pass_on)

    def forward_y(i):
        by_extra(i, lambda i, extra: gathered(i, extra).wait_recv())

        @pl.loop(0, CX)
        def _(k):
            x = CX * i + k

            def block_of(b):
                parts = []
                for pair in range(2):
                    first = jnp.where(pair == side, chip, 1 - chip)
                    at = pl.multiple_of(jnp.where(first == b, 0, ROWS), ROWS)
                    lines = r1[x, :, pair, :, pl.ds(at, ROWS), :]
                    parts.append(lines.reshape(NY // 2, LANES))
                return jnp.concatenate(parts, axis=0)

            both = jnp.concatenate([block_of(0), block_of(1)], axis=1)
            full = jnp.concatenate([both, turned_pair(both, sign)], axis=0)
            high, low = split(full)
            bh[...] = high
            bl[...] = low
            here, there = 2 * chip + core, 2 * chip + 1 - core
            y1[x] = product(fyh[there], fyl[there], bh[...], bl[...])
            r2[core, x] = product(fyh[here], fyl[here], bh[...], bl[...])

        quarters(i).start()

    def along_z(i):
        quarters(i).wait_recv()

        @pl.loop(0, CX // 2)
        def _(k):
            x = CX * i + 2 * k
            for j in range(2):
                line = jnp.concatenate([r2[0, x + j], r2[1, x + j]], axis=1)
                high, low = split(line)
                ah[j * YF : (j + 1) * YF] = high
                al[j * YF : (j + 1) * YF] = low
            for n in range(2):
                out = product(ah[...], al[...], wzh[n], wzl[n])
                for j in range(2):
                    lines = slice(j * YF, (j + 1) * YF)
                    real, imag = out[lines, :256], out[lines, 256:]
                    g_real = green[0, x + j, :, 256 * n : 256 * n + 256]
                    g_imag = green[1, x + j, :, 256 * n : 256 * n + 256]
                    high, low = split(real * g_real - imag * g_imag)
                    qh[lines, 512 * n : 512 * n + 256] = high
                    ql[lines, 512 * n : 512 * n + 256] = low
                    high, low = split(real * g_imag + imag * g_real)
                    qh[lines, 512 * n + 256 : 512 * n + 512] = high
                    ql[lines, 512 * n + 256 : 512 * n + 512] = low
            out = product(qh[...], ql[...], wih[1 - core], wil[1 - core])
            for j in range(2):
                zi[x + j] = out[j * YF : (j + 1) * YF]
            out = product(qh[...], ql[...], wih[core], wil[core])
            for j in range(2):
                r3[x + j, pl.ds(pl.multiple_of(YF * core, YF), YF), :] = out[
                    j * YF : (j + 1) * YF
                ]

        blocks(i).start()

    def inverse_y(i):
        blocks(i).wait_recv()

        @pl.loop(0, CX)
        def _(k):
            x = CX * i + k
            both = r3[x]
            full = jnp.concatenate([both, turned_pair(both, sign)], axis=0)
            high, low = split(full)
            bh[...] = high
            bl[...] = low
            out = product(fyih[chip], fyil[chip], bh[...], bl[...])
            for b in range(2):
                yp[b, x] = out[:, b * LANES : (b + 1) * LANES].reshape(4, 2, 32, LANES)

        for copy in partials(i):
            copy.start()

    def add_halves(i):
        for copy in partials(i):
            copy.wait_recv()

        @pl.loop(0, CX)
        def _(k):
            x = CX * i + k
            yi[0, x] = yp[chip, x, :, side] + yr[0, x]
            yi[1, x] = yp[1 - chip, x, :, 1 - side] + yr[1, x]

        def part(p):
            group, pair, rank = place(p)
            other = jnp.where(pair == side, 0, 1)
            first = pl.multiple_of(ROWS * rank, ROWS)
            return yi.at[other, pl.ds(CX * i, CX), group, pl.ds(first, ROWS)]

        mine = r4.at[i, pl.ds(CX * me, CX)]

        @pl.loop(1, GY)
        def _(k):
            p = lax.rem(me + k, GY)
            pltpu.make_async_remote_copy(
                src_ref=part(p),
                dst_ref=mine,
                send_sem=ss6.at[i],
                recv_sem=rs6.at[i],
                device_id=across(p),
                device_id_type=MESH,
            ).start()

        pltpu.make_async_copy(part(me), mine, rs6.at[i]).start()

    def inverse_x(last):
        j = last // JOIN
        for n in range(JOIN):
            whole = r4.at[JOIN * j + n]
            pltpu.make_async_copy(whole, whole, rs6.at[JOIN * j + n]).wait()
        lh, ll = fxih[j], fxil[j]

        def lines(y):
            return jnp.concatenate([r4[JOIN * j + n, :, y, :] for n in range(JOIN)], axis=0)

        for k in range(ROWS // 2):
            pair = jnp.concatenate([lines(2 * k), lines(2 * k + 1)], axis=1)
            full = jnp.concatenate([pair, turned_pair(pair, sign)], axis=0)
            high, low = split(full)
            acc[k] += product(lh, ll, high, low)

    def join_x(i):
        @pl.when(lax.rem(i, JOIN) == JOIN - 1)
        def _():
            inverse_x(i)

    acc[...] = jnp.zeros_like(acc)

    @pl.loop(0, CH + LAST)
    def _(step):
        def stage(lag, work):
            i = step - lag

            @pl.when((i >= 0) & (i < CH))
            def _():
                work(i)

        @pl.when(step == EARLY)
        def _():
            take_shared()

        stage(0, forward_x)

        @pl.when(step == 1)
        def _():
            for n in range(2, 12):
                fills[n].wait()
            loads[3].wait()

        stage(1, gather)
        stage(4, inverse_y)
        stage(3, along_z)
        stage(5, add_halves)
        stage(2, forward_y)
        stage(LAST, join_x)

        @pl.when(step == 2)
        def _():
            project()

    scale = 1.0 / float(PAD) ** 3

    @pl.loop(0, ROWS // 2)
    def _(k):
        for j in range(2):
            flat = acc[k, :, j * LANES : (j + 1) * LANES].T * scale
            adj[0, 2 * k + j] = src[0, 2 * k + j] - flat[:DEPTH]
            adj[1, 2 * k + j] = src[1, 2 * k + j] - flat[DEPTH:]

    loads[2].wait()
    holds = (mz == 1) | (mz == 2)
    slot = jnp.where(mz == 2, 1, 0)

    def slab_copy(step, turn):
        return pltpu.make_async_remote_copy(
            src_ref=slab,
            dst_ref=slabs.at[1 - step, slot],
            send_sem=sp.at[step + 1, turn],
            recv_sem=rp.at[1 - step, slot],
            device_id={
                "gy": lax.rem(me + GY + step, GY),
                "gz": lax.rem(mz + turn, GZ),
            },
            device_id_type=MESH,
        )

    reaches = [
        (step, turn) for step in (-1, 0, 1) for turn in range(GZ) if step or turn
    ]

    @pl.when(holds)
    def _():
        planes = pl.ds(slab_z, 16)
        field = adj[0, :, planes, :] * fwd[0] - adj[1, :, planes, :] * fwd[1]
        total = jnp.sum(field, axis=1) * (GAP / SLAB)
        slab[...] = total
        slabs[1, slot] = total
        for step, turn in reaches:
            slab_copy(step, turn).start()

    for copy in fact_copies:
        copy.wait()
    for step in range(3):
        for source in range(2):
            arrived = pltpu.make_async_copy(slab, slabs.at[step, source], rp.at[step, source])
            if step == 1:

                @pl.when(mz != source + 1)
                def _(arrived=arrived):
                    arrived.wait()

            else:
                arrived.wait()

    summed = [slabs[step, 0] + slabs[step, 1] for step in range(3)]
    sense = jnp.concatenate(
        [summed[0][ROWS - RADIUS :], summed[1], summed[2][:RADIUS]], axis=0
    )
    weighted = jnp.where(inside, wide(fact) * sense, 0.0)
    scaled = exact(weighted, filt[...]) / jnp.where(inside, weight16, 1.0)
    grad[...] = tent_rows(scaled)

    @pl.when(holds)
    def _():
        for step, turn in reaches:
            slab_copy(step, turn).wait_send()

    @pl.loop(0, CH)
    def _(i):
        def leave(i, extra):
            sent = s1.at[i, pl.ds(0, CX * (GY - 1)), pl.ds(0, ROWS + extra)]
            pltpu.make_async_copy(sent, sent, ss1.at[i]).wait()
            gathered(i, extra).wait_send()

        by_extra(i, leave)
        for copy in [quarters(i), blocks(i)] + partials(i):
            copy.wait_send()
        sent = r4.at[i, pl.ds(0, CX * (GY - 1))]
        pltpu.make_async_copy(sent, sent, ss6.at[i]).wait()


def hand_over(adj, proj, grad, adj_out, proj_out, grad_out):
    adj_out[...] = adj[...]
    proj_out[...] = proj[...]
    grad_out[...] = grad[...]


def shards(source, contrast, green, forward_field, density, thresh_index):
    constants = tables()
    anywhere = pl.BlockSpec(memory_space=pl.ANY)
    vmem = pl.BlockSpec(memory_space=pltpu.VMEM)
    dma = pltpu.SemaphoreType.DMA
    block = pltpu.VMEM
    scratch = [
        block((2, ROWS, DEPTH, NX), F32),
        block((ROWS, DEPTH, NX), F32),
        block((2, ROWS, 16, NX), F32),
        block((2, XF, YF, PAD), F32),
    ]
    scratch += [block(table.shape, table.dtype) for table in constants]
    scratch += [
        block((BOTH, 2 * NX, LANES), BF16),
        block((BOTH, 2 * NX, LANES), BF16),
        block((CH, GY * CX, 2 * ROWS, LANES), F32),
        block((XF, 4, 2, 4, 2 * ROWS, LANES), F32),
        block((XF, YF, 2 * LANES), F32),
        block((2, XF, YF, 2 * LANES), F32),
        block((XF, YF, 2 * LANES), F32),
        block((XF, 2 * YF, 2 * LANES), F32),
        block((2, XF, 4, 2, 32, LANES), F32),
        block((2, XF, 4, 32, LANES), F32),
        block((2, XF, 4, 32, LANES), F32),
        block((CH, GY * CX, ROWS, LANES), F32),
        block((ROWS // 2, NX, 2 * LANES), F32),
        block((PAD, 2 * LANES), BF16),
        block((PAD, 2 * LANES), BF16),
        block((2 * YF, 2 * NZ), BF16),
        block((2 * YF, 2 * NZ), BF16),
        block((2 * YF, 2 * PAD), BF16),
        block((2 * YF, 2 * PAD), BF16),
        block((3, ROWS, NX), F32),
        block((3, ROWS, NX), F32),
        block((ROWS, NX), F32),
        block((3, 2, ROWS, NX), F32),
        dma((4,)),
        dma((14,)),
    ]
    scratch += [dma((2,)) for _ in range(4)]
    scratch += [dma((3, GZ)), dma((3, 2))]
    scratch += [dma((CH,))] * 4
    scratch += [dma((CH,))] * 6 + [dma((CH, 2))] * 2 + [dma((CH,))] * 2
    scratch += [block((2, EXTRA, NX, LANES), F32), dma, dma]
    results = pl.pallas_call(
        kernel,
        out_shape=(
            jax.ShapeDtypeStruct((2, ROWS, DEPTH, NX), F32),
            jax.ShapeDtypeStruct((ROWS, NX), F32),
            jax.ShapeDtypeStruct((ROWS, NX), F32),
        ),
        in_specs=[anywhere] * 4 + [vmem] * 2 + [anywhere] * 14,
        out_specs=(vmem, vmem, vmem),
        scratch_shapes=scratch,
        compiler_params=pltpu.CompilerParams(
            collective_id=0, has_side_effects=True, vmem_limit_bytes=62 << 20
        ),
    )(source, contrast, forward_field, green, density, thresh_index, *map(jnp.asarray, constants))
    pieces = [pl.BlockSpec((2, ROWS // 4, DEPTH, NX), lambda n: (0, n, 0, 0))]
    pieces += [pl.BlockSpec((ROWS, NX), lambda n: (0, 0))] * 2
    return pl.pallas_call(
        hand_over,
        out_shape=tuple(jax.ShapeDtypeStruct(r.shape, r.dtype) for r in results),
        grid=(4,),
        in_specs=pieces,
        out_specs=tuple(pieces),
    )(*results)


def solution(mesh):
    return jax.shard_map(
        shards,
        mesh=mesh,
        in_specs=(
            P(None, "gy", "gz", None),
            P("gy", "gz", None),
            P(None, "gy", "gz", None),
            P(None, "gy", "gz", None),
            P("gy", None),
            P("gy", None),
        ),
        out_specs=(P(None, "gy", "gz", None), P("gy", None), P("gy", None)),
        check_vma=False,
    )
```

```python
import functools

import jax
import jax.numpy as jnp
import ml_dtypes
import numpy as np
from jax import lax
from jax.experimental import pallas as pl
from jax.experimental.pallas import tpu as pltpu
from jax.sharding import PartitionSpec as P

NX = NY = NZ = 256
PAD = 512
SLAB = 32
RADIUS = 4
TILE_Y = 4
TILE_X = 16
Z0 = 112
SHARP = 8.0
GAP = 11.0

GY = 32
GZ = 4
ROWS = NY // GY
DEPTH = NZ // GZ
XF = PAD // GY
YF = PAD // GZ
LANES = 2 * DEPTH
CH = 8
CX = XF // CH
EXTRA = 4
BOTH = ROWS + EXTRA
EARLY = 2
LAST = 7
JOIN = CH // 4

F32 = jnp.float32
BF16 = jnp.bfloat16
MESH = pl.DeviceIdType.MESH


def halves(table):
    high = table.astype(ml_dtypes.bfloat16)
    low = (table - high.astype(np.float64)).astype(ml_dtypes.bfloat16)
    return high, low


def tables():
    k = np.arange(PAD)[:, None]
    p = np.arange(NX)[None, :]
    angle = (k * p % PAD) * (2.0 * np.pi / PAD)
    cos, sin = np.cos(angle), np.sin(angle)
    order = np.arange(PAD).reshape(GY, CH, CX).transpose(1, 0, 2).reshape(CH, GY * CX)
    fx = np.concatenate([cos[order], sin[order]], axis=2)
    joined = order.reshape(CH // JOIN, JOIN * GY * CX)
    by_pair = np.arange(NY).reshape(4, 2, 32).transpose(1, 0, 2).reshape(NY)
    fy = np.concatenate([cos[:, by_pair], sin[:, by_pair]], axis=1)
    fy = fy.reshape(GZ, YF, 2 * NY)
    half = (2, PAD // 2, NY)
    fyi = np.concatenate(
        [cos.reshape(half).transpose(0, 2, 1), -sin.reshape(half).transpose(0, 2, 1)],
        axis=2,
    )
    fxi = np.concatenate(
        [cos[joined].transpose(0, 2, 1), -sin[joined].transpose(0, 2, 1)], axis=2
    )
    shape = (2, 256, 2, 2, DEPTH)
    ct = cos.reshape(shape).transpose(0, 3, 2, 4, 1)
    st = sin.reshape(shape).transpose(0, 3, 2, 4, 1)
    re_rows = np.concatenate([ct, -st], axis=4)
    im_rows = np.concatenate([st, ct], axis=4)
    wz = np.stack([re_rows, im_rows], axis=3).reshape(2, 2 * NZ, 512)
    wzi = wz.transpose(0, 2, 1).reshape(1024, 2, 256).transpose(1, 0, 2)
    flat = []
    for table in (fx, fy, fyi, fxi, wz, wzi):
        flat.extend(halves(table))
    cells = np.arange(NX)
    tent = np.maximum(RADIUS + 1 - np.abs(cells[:, None] - cells[None, :]), 0).astype(
        np.float32
    )
    filt = tent / tent.sum(axis=1, keepdims=True)
    return flat + [filt, np.ascontiguousarray(filt.T)]


def split(value):
    high = value.astype(BF16)
    return high, (value - high.astype(F32)).astype(BF16)


def product(ah, al, bh, bl):
    dot = functools.partial(jnp.dot, preferred_element_type=F32)
    return dot(ah, bh) + dot(al, bh) + dot(ah, bl)


def turned(block, sign):
    return pltpu.roll(block, DEPTH, 1) * sign


def turned_pair(pair, sign):
    return jnp.concatenate(
        [turned(pair[:, :LANES], sign), turned(pair[:, LANES:], sign)], axis=1
    )


def kernel(*refs):
    (src_h, con_h, fwd_h, green_h, dens, level) = refs[:6]
    tabs_h = refs[6:20]
    adj_h, proj, grad = refs[20:23]
    (src, con, fwd, green) = refs[23:27]
    tabs = refs[27:41]
    (sth, stl, s1, r1, y1, r2, zi, r3, yp, yr, yi, r4, acc) = refs[41:54]
    (raw, sw, rw, adj, out_sem) = refs[86:91]
    (bh, bl, ah, al, qh, ql, near, fact, slab, slabs) = refs[54:64]
    (in_sem, tab_sem, sn, rn, sf, rf, sp, rp) = refs[64:72]
    (ss1, rs1, ss2, rs2, ss3, rs3, _, ss4, rs4, _, ss5, rs5, ss6, rs6) = refs[72:86]
    fxh, fxl, fyh, fyl, fyih, fyil, fxih, fxil, wzh, wzl, wih, wil, filt, filt_t = tabs

    me = lax.axis_index("gy")
    mz = lax.axis_index("gz")
    after, before = lax.rem(me + 1, GY), lax.rem(me + GY - 1, GY)
    core, chip = lax.rem(mz, 2), mz // 2
    side = lax.rem(me // 4, 2)
    sibling = mz + 1 - 2 * core
    partner = lax.rem(mz + 2, GZ)

    def place(p):
        return p // 8, lax.rem(p // 4, 2), lax.rem(p, 4)

    def across(p):
        same = lax.rem(p // 4, 2) == side
        return {"gy": p, "gz": jnp.where(same, mz, partner)}

    slab_z = pl.multiple_of(jnp.where(mz == 1, 48, 0), 16)
    loads = [
        pltpu.make_async_copy(src_h, src, in_sem.at[0]),
        pltpu.make_async_copy(con_h, con, in_sem.at[1]),
        pltpu.make_async_copy(fwd_h.at[:, :, pl.ds(slab_z, 16), :], fwd, in_sem.at[2]),
        pltpu.make_async_copy(green_h, green, in_sem.at[3]),
    ]
    fills = [
        pltpu.make_async_copy(tabs_h[n], tabs[n], tab_sem.at[n]) for n in range(14)
    ]
    for copy in (loads[0], loads[1], fills[0], fills[1]):
        copy.start()

    barrier = pltpu.get_barrier_semaphore()

    @pl.loop(1, GY)
    def _(k):
        pl.semaphore_signal(
            barrier, inc=1, device_id=across(lax.rem(me + k, GY)), device_id_type=MESH
        )

    for k in range(GZ):
        other = lax.rem(mz + k, GZ)
        for row in (after, before) + ((me,) if k else ()):
            pl.semaphore_signal(
                barrier,
                inc=1,
                device_id={"gy": row, "gz": other},
                device_id_type=MESH,
            )

    lane = lax.broadcasted_iota(jnp.int32, (1, LANES), 1)
    sign = jnp.where(lane < DEPTH, 1.0, -1.0).astype(F32)

    loads[0].wait()
    loads[1].wait()
    for copy in fills[12:] + fills[2:6] + fills[8:12] + loads[3:] + fills[6:8] + loads[2:3]:
        copy.start()

    def stimulus(y):
        weight = con[y]
        both = jnp.concatenate([src[0, y] * weight, src[1, y] * weight], axis=0)
        return both.T

    def keep(y, flat):
        full = jnp.concatenate([flat, turned(flat, sign)], axis=0)
        high, low = split(full)
        sth[y] = high
        stl[y] = low

    @pl.loop(0, EXTRA)
    def _(y):
        raw[0, y] = stimulus(y)

    pl.semaphore_wait(barrier, (GY - 1) + 2 * GZ + (GZ - 1))

    shared = pltpu.make_async_remote_copy(
        src_ref=raw.at[0],
        dst_ref=raw.at[1],
        send_sem=sw,
        recv_sem=rw,
        device_id={"gz": partner},
        device_id_type=MESH,
    )
    shared.start()

    @pl.loop(0, EXTRA)
    def _(y):
        keep(y, raw[0, y])

    @pl.loop(EXTRA, ROWS)
    def _(y):
        keep(y, stimulus(y))

    fills[0].wait()
    fills[1].wait()

    def near_copy(buffer, slot, target, sems, recv):
        return pltpu.make_async_remote_copy(
            src_ref=buffer.at[2],
            dst_ref=buffer.at[slot],
            send_sem=sems.at[slot],
            recv_sem=recv.at[slot],
            device_id={"gy": target},
            device_id_type=MESH,
        )

    near[2] = dens[...]
    near_copies = [near_copy(near, 0, after, sn, rn), near_copy(near, 1, before, sn, rn)]
    for copy in near_copies:
        copy.start()

    def take_shared():
        shared.wait()

        @pl.loop(0, EXTRA)
        def _(y):
            keep(ROWS + y, raw[1, y])

    def by_extra(i, work):
        @pl.when(i < EARLY)
        def _():
            work(i, 0)

        @pl.when(i >= EARLY)
        def _():
            work(i, EXTRA)

    def forward_x(i):
        def rows(k):
            rh = jnp.concatenate([sth[2 * k], sth[2 * k + 1]], axis=1)
            rl = jnp.concatenate([stl[2 * k], stl[2 * k + 1]], axis=1)
            out = product(fxh[i], fxl[i], rh, rl)
            s1[i, :, 2 * k, :] = out[:, :LANES]
            s1[i, :, 2 * k + 1, :] = out[:, LANES:]

        for k in range(ROWS // 2):
            rows(k)

        @pl.when(i >= EARLY)
        def _():
            for k in range(ROWS // 2, BOTH // 2):
                rows(k)

        by_extra(i, spread_x)

    def spread_x(i, extra):
        count = pl.ds(0, ROWS + extra)

        def part(p):
            return s1.at[i, pl.ds(CX * p, CX), count]

        group, pair, rank = place(me)
        mine = r1.at[pl.ds(CX * i, CX), group, pair, rank, count]

        @pl.loop(1, GY)
        def _(k):
            p = lax.rem(me + k, GY)
            pltpu.make_async_remote_copy(
                src_ref=part(p),
                dst_ref=mine,
                send_sem=ss1.at[i],
                recv_sem=rs1.at[i],
                device_id=across(p),
                device_id_type=MESH,
            ).start()

        pltpu.make_async_copy(part(me), mine, rs1.at[i]).start()

    def wide(buffer):
        rows = jnp.concatenate(
            [buffer[0][ROWS - RADIUS :], buffer[2], buffer[1][:RADIUS]], axis=0
        )
        return jnp.where(inside, rows, 0.0)

    row = ROWS * me - RADIUS + lax.broadcasted_iota(jnp.int32, (2 * ROWS, NX), 0)
    inside = (row >= 0) & (row < NY)
    weight16 = jnp.zeros((2 * ROWS, NX), F32)
    for offset in range(-RADIUS, RADIUS + 1):
        valid = (row + offset >= 0) & (row + offset < NY)
        weight16 = weight16 + jnp.where(valid, float(RADIUS + 1 - abs(offset)), 0.0)

    def tent_rows(rows):
        total = jnp.zeros((ROWS, NX), F32)
        for offset in range(-RADIUS, RADIUS + 1):
            start = RADIUS + offset
            total = total + float(RADIUS + 1 - abs(offset)) * rows[start : start + ROWS]
        return total

    exact = functools.partial(
        jnp.dot, preferred_element_type=F32, precision=lax.Precision.HIGHEST
    )
    fact_copies = [near_copy(fact, 0, after, sf, rf), near_copy(fact, 1, before, sf, rf)]

    def project():
        fills[12].wait()
        fills[13].wait()
        for copy in near_copies:
            copy.wait()
        smooth = tent_rows(wide(near)) / weight16[RADIUS : RADIUS + ROWS]
        filtered = exact(smooth, filt_t[...])
        levels = 0.35 + 0.1 * level[...].astype(F32)
        tile = lax.broadcasted_iota(jnp.int32, (2, NX), 1) // TILE_X
        wide_levels = jnp.zeros((2, NX), F32)
        for n in range(NX // TILE_X):
            wide_levels = jnp.where(tile == n, levels[:, n : n + 1], wide_levels)
        upper = lax.broadcasted_iota(jnp.int32, (ROWS, NX), 0) < TILE_Y
        threshold = jnp.where(upper, wide_levels[0:1], wide_levels[1:2])
        steep = jnp.tanh(SHARP * (filtered - threshold))
        shift = jnp.tanh(SHARP * threshold)
        below = shift + jnp.tanh(SHARP * (1.0 - threshold))
        proj[...] = (shift + steep) / below
        fact[2] = SHARP * (1.0 - steep * steep) / below
        for copy in fact_copies:
            copy.start()

    def gathered(i, extra):
        lines = r1.at[pl.ds(CX * i, CX)]
        return pltpu.make_async_remote_copy(
            src_ref=lines.at[:, :, :, :, pl.ds(extra, ROWS - extra)],
            dst_ref=lines.at[:, :, :, :, pl.ds(ROWS + extra, ROWS - extra)],
            send_sem=ss2.at[i],
            recv_sem=rs2.at[i],
            device_id={"gz": partner},
            device_id_type=MESH,
        )

    def to_sibling(source, target, i, send, recv):
        return pltpu.make_async_remote_copy(
            src_ref=source,
            dst_ref=target,
            send_sem=send.at[i],
            recv_sem=recv.at[i],
            device_id={"gz": sibling},
            device_id_type=MESH,
        )

    def quarters(i):
        rows = pl.ds(CX * i, CX)
        return to_sibling(y1.at[rows], r2.at[core, rows], i, ss3, rs3)

    def blocks(i):
        rows = pl.ds(CX * i, CX)
        mine = r3.at[rows, pl.ds(pl.multiple_of(YF * core, YF), YF), :]
        return to_sibling(zi.at[rows], mine, i, ss4, rs4)

    def partials(i):
        rows = pl.ds(CX * i, CX)
        pieces = [yp.at[1 - chip, rows, :, side], yp.at[chip, rows, :, 1 - side]]
        return [
            pltpu.make_async_remote_copy(
                src_ref=pieces[n],
                dst_ref=yr.at[n, rows],
                send_sem=ss5.at[i, n],
                recv_sem=rs5.at[i, n],
                device_id={"gz": partner},
                device_id_type=MESH,
            )
            for n in range(2)
        ]

    def gather(i):
        def pass_on(i, extra):
            whole = r1.at[pl.ds(CX * i, CX), :, :, :, pl.ds(0, ROWS + extra)]
            pltpu.make_async_copy(whole, whole, rs1.at[i]).wait()
            gathered(i, extra).start()

        by_extra(i, pass_on)

    def forward_y(i):
        by_extra(i, lambda i, extra: gathered(i, extra).wait_recv())

        @pl.loop(0, CX)
        def _(k):
            x = CX * i + k

            def block_of(b):
                parts = []
                for pair in range(2):
                    first = jnp.where(pair == side, chip, 1 - chip)
                    at = pl.multiple_of(jnp.where(first == b, 0, ROWS), ROWS)
                    lines = r1[x, :, pair, :, pl.ds(at, ROWS), :]
                    parts.append(lines.reshape(NY // 2, LANES))
                return jnp.concatenate(parts, axis=0)

            both = jnp.concatenate([block_of(0), block_of(1)], axis=1)
            full = jnp.concatenate([both, turned_pair(both, sign)], axis=0)
            high, low = split(full)
            bh[...] = high
            bl[...] = low
            here, there = 2 * chip + core, 2 * chip + 1 - core
            y1[x] = product(fyh[there], fyl[there], bh[...], bl[...])
            r2[core, x] = product(fyh[here], fyl[here], bh[...], bl[...])

        quarters(i).start()

    def along_z(i):
        quarters(i).wait_recv()

        @pl.loop(0, CX // 2)
        def _(k):
            x = CX * i + 2 * k
            for j in range(2):
                line = jnp.concatenate([r2[0, x + j], r2[1, x + j]], axis=1)
                high, low = split(line)
                ah[j * YF : (j + 1) * YF] = high
                al[j * YF : (j + 1) * YF] = low
            for n in range(2):
                out = product(ah[...], al[...], wzh[n], wzl[n])
                for j in range(2):
                    lines = slice(j * YF, (j + 1) * YF)
                    real, imag = out[lines, :256], out[lines, 256:]
                    g_real = green[0, x + j, :, 256 * n : 256 * n + 256]
                    g_imag = green[1, x + j, :, 256 * n : 256 * n + 256]
                    high, low = split(real * g_real - imag * g_imag)
                    qh[lines, 512 * n : 512 * n + 256] = high
                    ql[lines, 512 * n : 512 * n + 256] = low
                    high, low = split(real * g_imag + imag * g_real)
                    qh[lines, 512 * n + 256 : 512 * n + 512] = high
                    ql[lines, 512 * n + 256 : 512 * n + 512] = low
            out = product(qh[...], ql[...], wih[1 - core], wil[1 - core])
            for j in range(2):
                zi[x + j] = out[j * YF : (j + 1) * YF]
            out = product(qh[...], ql[...], wih[core], wil[core])
            for j in range(2):
                r3[x + j, pl.ds(pl.multiple_of(YF * core, YF), YF), :] = out[
                    j * YF : (j + 1) * YF
                ]

        blocks(i).start()

    def inverse_y(i):
        blocks(i).wait_recv()

        @pl.loop(0, CX)
        def _(k):
            x = CX * i + k
            both = r3[x]
            full = jnp.concatenate([both, turned_pair(both, sign)], axis=0)
            high, low = split(full)
            bh[...] = high
            bl[...] = low
            out = product(fyih[chip], fyil[chip], bh[...], bl[...])
            for b in range(2):
                yp[b, x] = out[:, b * LANES : (b + 1) * LANES].reshape(4, 2, 32, LANES)

        for copy in partials(i):
            copy.start()

    def add_halves(i):
        for copy in partials(i):
            copy.wait_recv()

        @pl.loop(0, CX)
        def _(k):
            x = CX * i + k
            yi[0, x] = yp[chip, x, :, side] + yr[0, x]
            yi[1, x] = yp[1 - chip, x, :, 1 - side] + yr[1, x]

        def part(p):
            group, pair, rank = place(p)
            other = jnp.where(pair == side, 0, 1)
            first = pl.multiple_of(ROWS * rank, ROWS)
            return yi.at[other, pl.ds(CX * i, CX), group, pl.ds(first, ROWS)]

        mine = r4.at[i, pl.ds(CX * me, CX)]

        @pl.loop(1, GY)
        def _(k):
            p = lax.rem(me + k, GY)
            pltpu.make_async_remote_copy(
                src_ref=part(p),
                dst_ref=mine,
                send_sem=ss6.at[i],
                recv_sem=rs6.at[i],
                device_id=across(p),
                device_id_type=MESH,
            ).start()

        pltpu.make_async_copy(part(me), mine, rs6.at[i]).start()

    def inverse_x(last):
        j = last // JOIN
        for n in range(JOIN):
            whole = r4.at[JOIN * j + n]
            pltpu.make_async_copy(whole, whole, rs6.at[JOIN * j + n]).wait()
        lh, ll = fxih[j], fxil[j]

        def lines(y):
            return jnp.concatenate([r4[JOIN * j + n, :, y, :] for n in range(JOIN)], axis=0)

        for k in range(ROWS // 2):
            pair = jnp.concatenate([lines(2 * k), lines(2 * k + 1)], axis=1)
            full = jnp.concatenate([pair, turned_pair(pair, sign)], axis=0)
            high, low = split(full)
            acc[k] += product(lh, ll, high, low)

    def join_x(i):
        @pl.when(lax.rem(i, JOIN) == JOIN - 1)
        def _():
            inverse_x(i)

    acc[...] = jnp.zeros_like(acc)

    @pl.loop(0, CH + LAST)
    def _(step):
        def stage(lag, work):
            i = step - lag

            @pl.when((i >= 0) & (i < CH))
            def _():
                work(i)

        @pl.when(step == EARLY)
        def _():
            take_shared()

        stage(0, forward_x)

        @pl.when(step == 1)
        def _():
            for n in range(2, 12):
                fills[n].wait()
            loads[3].wait()

        stage(1, gather)
        stage(4, inverse_y)
        stage(3, along_z)
        stage(6, add_halves)
        stage(2, forward_y)
        stage(LAST, join_x)

        @pl.when(step == 2)
        def _():
            project()

    scale = 1.0 / float(PAD) ** 3

    @pl.loop(0, ROWS // 2)
    def _(k):
        for j in range(2):
            flat = acc[k, :, j * LANES : (j + 1) * LANES].T * scale
            adj[0, 2 * k + j] = src[0, 2 * k + j] - flat[:DEPTH]
            adj[1, 2 * k + j] = src[1, 2 * k + j] - flat[DEPTH:]

    done = pltpu.make_async_copy(adj, adj_h, out_sem)
    done.start()

    loads[2].wait()
    holds = (mz == 1) | (mz == 2)
    slot = jnp.where(mz == 2, 1, 0)

    def slab_copy(step, turn):
        return pltpu.make_async_remote_copy(
            src_ref=slab,
            dst_ref=slabs.at[1 - step, slot],
            send_sem=sp.at[step + 1, turn],
            recv_sem=rp.at[1 - step, slot],
            device_id={
                "gy": lax.rem(me + GY + step, GY),
                "gz": lax.rem(mz + turn, GZ),
            },
            device_id_type=MESH,
        )

    reaches = [
        (step, turn) for step in (-1, 0, 1) for turn in range(GZ) if step or turn
    ]

    @pl.when(holds)
    def _():
        planes = pl.ds(slab_z, 16)
        field = adj[0, :, planes, :] * fwd[0] - adj[1, :, planes, :] * fwd[1]
        total = jnp.sum(field, axis=1) * (GAP / SLAB)
        slab[...] = total
        slabs[1, slot] = total
        for step, turn in reaches:
            slab_copy(step, turn).start()

    for copy in fact_copies:
        copy.wait()
    for step in range(3):
        for source in range(2):
            arrived = pltpu.make_async_copy(slab, slabs.at[step, source], rp.at[step, source])
            if step == 1:

                @pl.when(mz != source + 1)
                def _(arrived=arrived):
                    arrived.wait()

            else:
                arrived.wait()

    summed = [slabs[step, 0] + slabs[step, 1] for step in range(3)]
    sense = jnp.concatenate(
        [summed[0][ROWS - RADIUS :], summed[1], summed[2][:RADIUS]], axis=0
    )
    weighted = jnp.where(inside, wide(fact) * sense, 0.0)
    scaled = exact(weighted, filt[...]) / jnp.where(inside, weight16, 1.0)
    grad[...] = tent_rows(scaled)

    @pl.when(holds)
    def _():
        for step, turn in reaches:
            slab_copy(step, turn).wait_send()

    done.wait()

    @pl.loop(0, CH)
    def _(i):
        def leave(i, extra):
            sent = s1.at[i, pl.ds(0, CX * (GY - 1)), pl.ds(0, ROWS + extra)]
            pltpu.make_async_copy(sent, sent, ss1.at[i]).wait()
            gathered(i, extra).wait_send()

        by_extra(i, leave)
        for copy in [quarters(i), blocks(i)] + partials(i):
            copy.wait_send()
        sent = r4.at[i, pl.ds(0, CX * (GY - 1))]
        pltpu.make_async_copy(sent, sent, ss6.at[i]).wait()


def hand_over(adj, proj, grad, adj_out, proj_out, grad_out):
    adj_out[...] = adj[...]
    proj_out[...] = proj[...]
    grad_out[...] = grad[...]


def shards(source, contrast, green, forward_field, density, thresh_index):
    constants = tables()
    anywhere = pl.BlockSpec(memory_space=pl.ANY)
    vmem = pl.BlockSpec(memory_space=pltpu.VMEM)
    dma = pltpu.SemaphoreType.DMA
    block = pltpu.VMEM
    scratch = [
        block((2, ROWS, DEPTH, NX), F32),
        block((ROWS, DEPTH, NX), F32),
        block((2, ROWS, 16, NX), F32),
        block((2, XF, YF, PAD), F32),
    ]
    scratch += [block(table.shape, table.dtype) for table in constants]
    scratch += [
        block((BOTH, 2 * NX, LANES), BF16),
        block((BOTH, 2 * NX, LANES), BF16),
        block((CH, GY * CX, 2 * ROWS, LANES), F32),
        block((XF, 4, 2, 4, 2 * ROWS, LANES), F32),
        block((XF, YF, 2 * LANES), F32),
        block((2, XF, YF, 2 * LANES), F32),
        block((XF, YF, 2 * LANES), F32),
        block((XF, 2 * YF, 2 * LANES), F32),
        block((2, XF, 4, 2, 32, LANES), F32),
        block((2, XF, 4, 32, LANES), F32),
        block((2, XF, 4, 32, LANES), F32),
        block((CH, GY * CX, ROWS, LANES), F32),
        block((ROWS // 2, NX, 2 * LANES), F32),
        block((PAD, 2 * LANES), BF16),
        block((PAD, 2 * LANES), BF16),
        block((2 * YF, 2 * NZ), BF16),
        block((2 * YF, 2 * NZ), BF16),
        block((2 * YF, 2 * PAD), BF16),
        block((2 * YF, 2 * PAD), BF16),
        block((3, ROWS, NX), F32),
        block((3, ROWS, NX), F32),
        block((ROWS, NX), F32),
        block((3, 2, ROWS, NX), F32),
        dma((4,)),
        dma((14,)),
    ]
    scratch += [dma((2,)) for _ in range(4)]
    scratch += [dma((3, GZ)), dma((3, 2))]
    scratch += [dma((CH,))] * 4
    scratch += [dma((CH,))] * 6 + [dma((CH, 2))] * 2 + [dma((CH,))] * 2
    scratch += [block((2, EXTRA, NX, LANES), F32), dma, dma]
    scratch += [block((2, ROWS, DEPTH, NX), F32), dma]
    results = pl.pallas_call(
        kernel,
        out_shape=(
            jax.ShapeDtypeStruct((2, ROWS, DEPTH, NX), F32),
            jax.ShapeDtypeStruct((ROWS, NX), F32),
            jax.ShapeDtypeStruct((ROWS, NX), F32),
        ),
        in_specs=[anywhere] * 4 + [vmem] * 2 + [anywhere] * 14,
        out_specs=(anywhere, vmem, vmem),
        scratch_shapes=scratch,
        compiler_params=pltpu.CompilerParams(
            collective_id=0, has_side_effects=True, vmem_limit_bytes=62 << 20
        ),
    )(source, contrast, forward_field, green, density, thresh_index, *map(jnp.asarray, constants))
    pieces = [pl.BlockSpec((2, ROWS // 4, DEPTH, NX), lambda n: (0, n, 0, 0))]
    pieces += [pl.BlockSpec((ROWS, NX), lambda n: (0, 0))] * 2
    return pl.pallas_call(
        hand_over,
        out_shape=tuple(jax.ShapeDtypeStruct(r.shape, r.dtype) for r in results),
        grid=(4,),
        in_specs=pieces,
        out_specs=tuple(pieces),
    )(*results)


def solution(mesh):
    return jax.shard_map(
        shards,
        mesh=mesh,
        in_specs=(
            P(None, "gy", "gz", None),
            P("gy", "gz", None),
            P(None, "gy", "gz", None),
            P(None, "gy", "gz", None),
            P("gy", None),
            P("gy", None),
        ),
        out_specs=(P(None, "gy", "gz", None), P("gy", None), P("gy", None)),
        check_vma=False,
    )
```
